32 devices in a mesh: ctx: 16 (over z, x, core), dp: 2 (over y).
Axes of the slice: x: 2, y: 2, z: 4, core: 2. Of those that a mesh axis runs over, the one named last changes fastest.
Arguments:
- query_proj: bfloat16 [2, 2048, 1024], P('dp', 'ctx'), may hold values from -6 to 6
- key_proj: bfloat16 [2, 2048, 1024], P('dp', 'ctx'), may hold values from -6 to 6
- value_proj: bfloat16 [2, 2048, 1024], P('dp', 'ctx'), may hold values from -6 to 6
- grad_out: bfloat16 [2, 2048, 4096], P('dp', 'ctx'), may hold values from -6 to 6
- out_weight: bfloat16 [1024, 4096], P('ctx'), may hold values from -0.1875 to 0.1875
- short_taps: float32 [3, 1024, 7], replicated, may hold values from -2 to 2
- residues: float32 [1024, 16], replicated, may hold values from -1.5 to 1.5
- decay_rate: float32 [1024, 16], replicated, may hold values from 0.00012207031 to 0.05
Outputs:
- grad_query: bfloat16 [2, 2048, 1024], P('dp', 'ctx')
- grad_key: bfloat16 [2, 2048, 1024], P('dp', 'ctx')
- grad_value: bfloat16 [2, 2048, 1024], P('dp', 'ctx')
- weight_grad: float32 [1024, 4096], P('ctx')
- taps_grad: float32 [3, 1024, 7], replicated
- residue_grad: float32 [1024, 16], replicated
The draws below stay inside these ranges and needn't reach their ends.
All inputs are finite; a program needn't handle non-finite values.
Results may differ from the reference program's by a relative error of at most 0.0075.
Values may be sent and summed in bfloat16 or wider, within the bound.
A program may use at most 192 MiB of HBM per device.

```python
import math
import jax
import jax.numpy as jnp
from jax import lax

C = 1024
D = 4096
M = 16
L = 2048
BATCH = 2


def level_of(stream_key, extent, cuts, smallest, largest):
    def one(position, parts):
        heights = jax.random.uniform(jax.random.fold_in(jax.random.fold_in(stream_key, 6), position), (parts,), jnp.float32, smallest / len(cuts), largest / len(cuts))
        return jnp.repeat(jnp.exp(heights), extent[position] // parts).reshape((-1,) + (1,) * (len(extent) - position - 1))

    level = one(*cuts[0])
    for cut in cuts[1:]:
        level = level * one(*cut)
    return level


def noise(own_key, shape, spread, reach, pieces=(), dtype=jnp.bfloat16):
    values = jax.random.normal(own_key, shape, jnp.float32) * spread
    if len(pieces) > 0:
        values = level_of(own_key, shape, pieces, -0.22, 0.18) * values
    return jnp.clip(values, min=-reach, max=reach).astype(dtype)


def setup_inputs(seed: int = 0) -> dict:
    arg_keys = jax.random.split(jax.random.key(seed), 9)
    return {
        "query_proj": noise(arg_keys[0], (BATCH, L, C), 1.0, 6.0, ((0, 2), (1, 16))),
        "key_proj": noise(arg_keys[1], (BATCH, L, C), 1.0, 6.0, ((0, 2), (1, 16))),
        "value_proj": noise(arg_keys[2], (BATCH, L, C), 1.0, 6.0, ((0, 2), (1, 16))),
        "grad_out": noise(arg_keys[3], (BATCH, L, D), 1.0, 6.0, ((0, 2), (1, 16))),
        "out_weight": noise(arg_keys[4], (C, D), C ** -0.5, 0.1875, ((0, 16),)),
        "short_taps": noise(arg_keys[5], (3, C, 7), 7 ** -0.5, 2.0, (), jnp.float32),
        "residues": noise(arg_keys[6], (C, M), M ** -0.5, 1.5, (), jnp.float32),
        "decay_rate": jnp.clip(jnp.exp(jax.random.uniform(arg_keys[7], (C, M), jnp.float32, math.log(0.00012207031), math.log(0.05))), 0.00012207031, 0.05),
    }


def shift_sum(field, taps):
    length = field.shape[1]
    padded = jnp.pad(field, ((0, 0), (6, 0), (0, 0)))
    result = jnp.zeros_like(field)
    for lag in range(7):
        result = result + taps[:, lag] * padded[:, 6 - lag:6 - lag + length, :]
    return result

def adjoint_sum(grad, taps):
    length = grad.shape[1]
    padded = jnp.pad(grad, ((0, 0), (0, 6), (0, 0)))
    result = jnp.zeros_like(grad)
    for lag in range(7):
        result = result + taps[:, lag] * padded[:, lag:lag + length, :]
    return result

def tap_terms(grad, field):
    length = field.shape[1]
    padded = jnp.pad(field, ((0, 0), (6, 0), (0, 0)))
    return jnp.stack([lax.optimization_barrier(jnp.sum(grad * padded[:, 6 - lag:6 - lag + length, :], axis=(0, 1))) for lag in range(7)], axis=-1)

def reference(query_proj, key_proj, value_proj, grad_out, out_weight, short_taps, residues, decay_rate):
    query_f = query_proj.astype(jnp.float32)
    key_f = key_proj.astype(jnp.float32)
    value_f = value_proj.astype(jnp.float32)
    shaped_q = shift_sum(query_f, short_taps[0])
    shaped_k = shift_sum(key_f, short_taps[1])
    shaped_v = shift_sum(value_f, short_taps[2])
    mixed = shaped_k * shaped_v
    factor = jnp.exp(-decay_rate)
    norm = jnp.sqrt(-jnp.expm1(-2.0 * decay_rate))
    coef = residues * norm
    start = jnp.zeros((BATCH, C, M), jnp.float32)

    def forward_step(state, column):
        state = factor * state + column[:, :, None]
        return (state, lax.optimization_barrier(jnp.sum(coef * state, axis=-1)))
    _, filtered = lax.scan(forward_step, start, jnp.swapaxes(mixed, 0, 1))
    filtered = jnp.swapaxes(filtered, 0, 1)
    flat_out = grad_out.reshape(-1, D)
    upstream = jnp.dot(flat_out, out_weight.T, preferred_element_type=jnp.float32).reshape(BATCH, -1, C)
    gated = (shaped_q * filtered).astype(jnp.bfloat16)
    weight_grad = jnp.dot(gated.reshape(-1, C).T, flat_out, preferred_element_type=jnp.float32)
    grad_filtered = upstream * shaped_q
    grad_qs = upstream * filtered

    def backward_step(carry, columns):
        adjoint, total = carry
        grad_col, mix_col = columns
        adjoint = factor * adjoint + grad_col[:, :, None]
        total = total + mix_col[:, :, None] * adjoint
        return ((adjoint, total), lax.optimization_barrier(jnp.sum(coef * adjoint, axis=-1)))
    (_, total), grad_mixed = lax.scan(backward_step, (start, start), (jnp.swapaxes(grad_filtered, 0, 1), jnp.swapaxes(mixed, 0, 1)), reverse=True)
    grad_mixed = jnp.swapaxes(grad_mixed, 0, 1)
    residue_grad = norm * lax.optimization_barrier(jnp.sum(total, axis=0))
    grad_ks = grad_mixed * shaped_v
    grad_vs = grad_mixed * shaped_k
    grad_query = adjoint_sum(grad_qs, short_taps[0]).astype(jnp.bfloat16)
    grad_key = adjoint_sum(grad_ks, short_taps[1]).astype(jnp.bfloat16)
    grad_value = adjoint_sum(grad_vs, short_taps[2]).astype(jnp.bfloat16)
    taps_grad = jnp.stack([tap_terms(grad_qs, query_f), tap_terms(grad_ks, key_f), tap_terms(grad_vs, value_f)])
    return (grad_query, grad_key, grad_value, weight_grad, taps_grad, residue_grad)
```

```python
import functools
import math

import jax
import jax.numpy as jnp
from jax import lax
from jax.experimental import pallas as pl
from jax.experimental.pallas import tpu as pltpu
from jax.sharding import PartitionSpec as P

LANES = 128
CHUNKS = 8
HALO = 8


def at_device(ctx, dp=None):
    return {"ctx": ctx} if dp is None else {"ctx": ctx, "dp": dp}


def greet_all(ctx_count, dp_count):
    barrier = pltpu.get_barrier_semaphore()
    me, row = lax.axis_index("ctx"), lax.axis_index("dp")
    for step in range(ctx_count):
        for other in range(dp_count):
            if step + other > 0:
                pl.semaphore_signal(
                    barrier,
                    inc=1,
                    device_id=at_device(
                        lax.rem(me + step, ctx_count),
                        None if dp_count == 1 else lax.rem(row + other, dp_count),
                    ),
                    device_id_type=pl.DeviceIdType.MESH,
                )
    pl.semaphore_wait(barrier, ctx_count * dp_count - 1)


def remote(src, dst, send, recv, ctx, dp=None):
    return pltpu.make_async_remote_copy(
        src_ref=src,
        dst_ref=dst,
        send_sem=send,
        recv_sem=recv,
        device_id=at_device(ctx, dp),
        device_id_type=pl.DeviceIdType.MESH,
    )


def gather_kernel(
    group, count, x_ref, go_ref, w_ref, xg_ref, gog_ref, wg_ref, halo_ref,
    xs, xr, gs, gr, ws, wr, hs, hr, own,
):
    me = lax.axis_index("ctx")
    mine, block = lax.rem(me, group), lax.div(me, group)
    tokens = go_ref.shape[0]
    greet_all(group * count, 1)
    sends = []
    for step in range(1, count):
        there = lax.rem(block + step, count)
        sends.append(
            remote(w_ref, wg_ref.at[block], ws.at[step], wr.at[step], there * group + mine)
        )
    for step in range(1, group):
        there = lax.rem(mine + step, group)
        to = block * group + there
        sends.append(remote(x_ref.at[there], xg_ref.at[mine], xs.at[step], xr.at[step], to))
        sends.append(remote(go_ref, gog_ref.at[mine], gs.at[step], gr.at[step], to))
    for copy in sends:
        copy.start()

    def halo_copy(there):
        ahead = jnp.minimum(block + 1, count - 1)
        return remote(
            x_ref.at[there, :, pl.ds(tokens - 16, 16), :],
            halo_ref,
            hs.at[there],
            hr.at[0],
            ahead * group + there,
        )

    @pl.when((mine == group - 1) & (block < count - 1))
    def _():
        for there in range(group):
            halo_copy(there).start()

    locals_ = [
        pltpu.make_async_copy(x_ref.at[mine], xg_ref.at[mine], own.at[0]),
        pltpu.make_async_copy(go_ref, gog_ref.at[mine], own.at[1]),
        pltpu.make_async_copy(w_ref, wg_ref.at[block], own.at[2]),
    ]
    for copy in locals_:
        copy.start()
    for copy in locals_:
        copy.wait()

    @pl.when(block == 0)
    def _():
        halo_ref[...] = jnp.zeros_like(halo_ref)

    for copy in sends:
        copy.wait()

    @pl.when((mine == group - 1) & (block < count - 1))
    def _():
        for there in range(group):
            halo_copy(there).wait_send()

    @pl.when(block > 0)
    def _():
        halo_copy(0).wait_recv()


def tree_sum(parts):
    parts = list(parts)
    while len(parts) > 1:
        parts = [
            parts[k] + parts[k + 1] if k + 1 < len(parts) else parts[k]
            for k in range(0, len(parts), 2)
        ]
    return parts[0]


def scan_kernel(
    group, count, x_ref, up_ref, taps_ref, factor_ref, coef_ref, chunk_ref, whole_ref,
    fore_ref, back_ref, norm_ref, y_ref, gated_ref, small_ref,
    shaped, mixed, gradf, gext, starts, bstarts, states, hsend, hrecv,
    ss, sr, hss, hsr,
):
    me = lax.axis_index("ctx")
    mine, block = lax.rem(me, group), lax.div(me, group)
    steps = up_ref.shape[0]
    width = up_ref.shape[2]
    modes = factor_ref.shape[0]
    greet_all(group * count, 1)
    row = lax.broadcasted_iota(jnp.int32, (CHUNKS, LANES), 0)
    spans = [slice(k, k + LANES) for k in range(0, width, LANES)]

    def down(v):
        return jnp.where(row > 0, pltpu.roll(v, 1, 0), 0.0)

    def up(v):
        return jnp.where(row < CHUNKS - 1, pltpu.roll(v, CHUNKS - 1, 0), 0.0)

    zeros = tuple(jnp.zeros((CHUNKS, LANES), jnp.float32) for _ in range(modes))
    for span in spans:

        def first(s, state):
            made = []
            for i in range(3):
                total = tree_sum(
                    [taps_ref[i, j, :, span] * x_ref[i, s + HALO - j, :, span] for j in range(7)]
                )
                shaped[i, s, :, span] = total
                made.append(total)
            value = made[1] * made[2]
            mixed[s, :, span] = value
            gradf[s, :, span] = up_ref[s, :, span] * made[0]
            return tuple(factor_ref[m, :, span] * state[m] + value for m in range(modes))

        ends = lax.fori_loop(0, steps, first, zeros)

        def first_back(k, state):
            value = gradf[steps - 1 - k, :, span]
            return tuple(factor_ref[m, :, span] * state[m] + value for m in range(modes))

        firsts = lax.fori_loop(0, steps, first_back, zeros)
        for m in range(modes):
            fs = chunk_ref[m, :, span]
            a = jnp.zeros((CHUNKS, LANES), jnp.float32)
            b = a
            for _ in range(CHUNKS - 1):
                a = down(fs * a + ends[m])
                b = up(fs * b + firsts[m])
            starts[m, :, span] = a
            bstarts[m, :, span] = b
            states[block, 0, m : m + 1, span] = (fs * a + ends[m])[CHUNKS - 1 :]
            states[block, 1, m : m + 1, span] = (fs * b + firsts[m])[:1]

    copies = [
        remote(
            states.at[block],
            states.at[block],
            ss.at[step],
            sr.at[step],
            lax.rem(block + step, count) * group + mine,
        )
        for step in range(1, count)
    ]
    for copy in copies:
        copy.start()
    for copy in copies:
        copy.wait()
    incoming = jnp.zeros((modes, width), jnp.float32)
    outgoing = incoming
    decay = whole_ref[...]
    for k in range(count):
        incoming = jnp.where(k < block, decay * incoming + states[k, 0], incoming)
        r = count - 1 - k
        outgoing = jnp.where(r > block, decay * outgoing + states[r, 1], outgoing)
    for span in spans:
        for m in range(modes):
            starts[m, :, span] += fore_ref[m, :, span] * incoming[m : m + 1, span]
            bstarts[m, :, span] += back_ref[m, :, span] * outgoing[m : m + 1, span]

    for span in spans:

        def second(s, state):
            value = mixed[s, :, span]
            new = tuple(factor_ref[m, :, span] * state[m] + value for m in range(modes))
            filtered = tree_sum([coef_ref[m, :, span] * new[m] for m in range(modes)])
            gated_ref[s, :, span] = shaped[0, s, :, span] * filtered
            gext[0, s, :, span] = up_ref[s, :, span] * filtered
            return new

        lax.fori_loop(0, steps, second, tuple(starts[m, :, span] for m in range(modes)))

        def second_back(k, carry):
            state, total = carry
            s = steps - 1 - k
            value = gradf[s, :, span]
            other = mixed[s, :, span]
            new = tuple(factor_ref[m, :, span] * state[m] + value for m in range(modes))
            total = tuple(total[m] + other * new[m] for m in range(modes))
            grad = tree_sum([coef_ref[m, :, span] * new[m] for m in range(modes)])
            gext[1, s, :, span] = grad * shaped[2, s, :, span]
            gext[2, s, :, span] = grad * shaped[1, s, :, span]
            return new, total

        _, total = lax.fori_loop(
            0, steps, second_back, (tuple(bstarts[m, :, span] for m in range(modes)), zeros)
        )
        for m in range(modes):
            small_ref[21 + m : 22 + m, span] = norm_ref[m : m + 1, span] * jnp.sum(
                total[m], axis=0, keepdims=True
            )
    small_ref[21 + modes :, :] = jnp.zeros((small_ref.shape[0] - 21 - modes, width), jnp.float32)

    for i in range(3):
        for s in range(HALO):
            hsend[i, s : s + 1, :] = gext[i, s, 0:1, :]
    ahead = remote(
        hsend, hrecv, hss.at[0], hsr.at[0], jnp.maximum(block - 1, 0) * group + mine
    )

    @pl.when(block > 0)
    def _():
        ahead.start()

    for span in spans:
        for i in range(3):

            def tap(s, sums):
                value = gext[i, s, :, span]
                return tuple(
                    sums[j] + value * x_ref[i, s + HALO - j, :, span] for j in range(7)
                )

            sums = lax.fori_loop(0, steps, tap, zeros[:7], unroll=2)
            for j in range(7):
                at = i * 7 + j
                small_ref[at : at + 1, span] = jnp.sum(sums[j], axis=0, keepdims=True)

    @pl.when(block == count - 1)
    def _():
        hrecv[...] = jnp.zeros_like(hrecv)

    @pl.when(block > 0)
    def _():
        ahead.wait_send()

    @pl.when(block < count - 1)
    def _():
        ahead.wait_recv()

    for span in spans:
        for i in range(3):
            for s in range(HALO):
                gext[i, steps + s, :, span] = jnp.where(
                    row < CHUNKS - 1,
                    pltpu.roll(gext[i, s, :, span], CHUNKS - 1, 0),
                    hrecv[i, s : s + 1, span],
                )

            def out(s, nothing):
                y_ref[i, s, :, span] = tree_sum(
                    [taps_ref[i, j, :, span] * gext[i, s + j, :, span] for j in range(7)]
                )
                return nothing

            lax.fori_loop(0, steps, out, 0, unroll=2)


def exchange_kernel(
    group, count, rows_dp, wp_ref, y_ref, small_ref, wg_ref, yo_ref, so_ref,
    wbuf, pair, sbuf, wsend, wrecv, ysend, yrecv, ssend, srecv, tsend, trecv, psend, precv, own,
):
    me, row = lax.axis_index("ctx"), lax.axis_index("dp")
    mine, block = lax.rem(me, group), lax.div(me, group)
    greet_all(group * count, rows_dp)
    weights, outs, smalls, totals, pairs = [], [], [], [], []
    members = count * rows_dp
    slot = block * rows_dp + row
    for step in range(1, members):
        there = lax.rem(slot + step, members)
        smalls.append(
            remote(
                small_ref,
                sbuf.at[slot],
                ssend.at[step],
                srecv.at[step],
                lax.div(there, rows_dp) * group + mine,
                lax.rem(there, rows_dp),
            )
        )
    for step in range(1, count):
        there = lax.rem(block + step, count)
        weights.append(
            remote(
                wp_ref.at[there], wbuf.at[step], wsend.at[step], wrecv.at[step],
                there * group + mine,
            )
        )
    for step in range(1, group):
        there = lax.rem(mine + step, group)
        to = block * group + there
        outs.append(
            remote(y_ref.at[there], yo_ref.at[mine], ysend.at[step], yrecv.at[step], to)
        )
        totals.append(
            remote(so_ref.at[mine], so_ref.at[mine], tsend.at[step], trecv.at[step], to)
        )
    for copy in smalls + weights + outs:
        copy.start()
    keep = pltpu.make_async_copy(y_ref.at[mine], yo_ref.at[mine], own.at[0])
    keep.start()
    sbuf[slot] = small_ref[...]
    for copy in smalls:
        copy.wait()
    total = sbuf[0]
    for k in range(1, members):
        total = total + sbuf[k]
    so_ref[mine] = total
    for copy in totals:
        copy.start()
    for copy in weights:
        copy.wait()
    columns = wg_ref.shape[1]
    tile = math.gcd(columns, 512)

    def add(k, nothing):
        at = pl.ds(pl.multiple_of(k * tile, tile), tile)
        value = wp_ref[block, :, at].astype(jnp.float32)
        for step in range(1, count):
            value = value + wbuf[step, :, at].astype(jnp.float32)
        pair[row, :, at] = value.astype(pair.dtype)
        return nothing

    lax.fori_loop(0, columns // tile, add, 0)
    for step in range(1, rows_dp):
        pairs.append(
            remote(
                pair.at[row], pair.at[row], psend.at[step], precv.at[step],
                me, lax.rem(row + step, rows_dp),
            )
        )
    for copy in pairs:
        copy.start()
    for copy in pairs:
        copy.wait()

    def finish(k, nothing):
        at = pl.ds(pl.multiple_of(k * tile, tile), tile)
        value = pair[0, :, at].astype(jnp.float32)
        for other in range(1, rows_dp):
            value = value + pair[other, :, at].astype(jnp.float32)
        wg_ref[:, at] = value
        return nothing

    lax.fori_loop(0, columns // tile, finish, 0)
    keep.wait()
    for copy in outs + totals:
        copy.wait()


VMEM = pl.BlockSpec(memory_space=pltpu.VMEM)
DMA = pltpu.SemaphoreType.DMA


def params(number):
    return pltpu.CompilerParams(
        collective_id=number, has_side_effects=True, vmem_limit_bytes=56 * 1024 * 1024
    )


def shards(
    query_proj, key_proj, value_proj, grad_out, out_weight, short_taps, residues, decay_rate
):
    devices, rows_dp = lax.axis_size("ctx"), lax.axis_size("dp")
    group = math.gcd(devices, 4)
    count = devices // group
    mine = lax.rem(lax.axis_index("ctx"), group)
    tokens, channels = query_proj.shape[1:]
    own_rows, columns = out_weight.shape
    width = count * own_rows
    modes = residues.shape[1]
    span_tokens = group * tokens
    steps = span_tokens // CHUNKS
    f32, bf16 = jnp.float32, jnp.bfloat16

    def parted(v):
        v = v.reshape(v.shape[:-1] + (count, group, own_rows))
        return jnp.moveaxis(v, -2, 0).reshape((group,) + v.shape[:-3] + (width,))

    def picked(v):
        return lax.dynamic_index_in_dim(parted(v), mine, 0, keepdims=False)

    streams = parted(jnp.stack([query_proj[0], key_proj[0], value_proj[0]]))
    xg, gog, wg, halo = pl.pallas_call(
        functools.partial(gather_kernel, group, count),
        out_shape=(
            jax.ShapeDtypeStruct((group, 3, tokens, width), bf16),
            jax.ShapeDtypeStruct((group, tokens, columns), bf16),
            jax.ShapeDtypeStruct((count, own_rows, columns), bf16),
            jax.ShapeDtypeStruct((3, 16, width), bf16),
        ),
        in_specs=[VMEM] * 3,
        out_specs=(VMEM,) * 4,
        scratch_shapes=[
            DMA((group,)), DMA((group,)), DMA((group,)), DMA((group,)),
            DMA((count,)), DMA((count,)), DMA((group,)), DMA((1,)), DMA((3,)),
        ],
        compiler_params=params(0),
        name="gather",
    )(streams, grad_out[0], out_weight)

    out_rows = gog.reshape(span_tokens, columns)
    upstream = lax.dot_general(
        out_rows,
        wg.reshape(width, columns),
        (((1,), (1,)), ((), ())),
        preferred_element_type=f32,
    )
    upstream = jnp.swapaxes(upstream.reshape(CHUNKS, steps, width), 0, 1)
    whole = jnp.swapaxes(xg, 0, 1).reshape(3, CHUNKS, steps, width)
    before = jnp.concatenate(
        [halo[:, None, 16 - HALO :], whole[:, :-1, steps - HALO :]], axis=1
    )
    extended = jnp.swapaxes(jnp.concatenate([before, whole], axis=2), 1, 2).astype(f32)

    taps = picked(jnp.swapaxes(short_taps, 1, 2))
    rate = picked(decay_rate.T)
    norm = jnp.sqrt(-jnp.expm1(-2.0 * rate))
    coef = picked(residues.T) * norm
    places = jnp.arange(CHUNKS, dtype=f32)[None, :, None]

    def spread(v):
        return jnp.broadcast_to(v[..., None, :], v.shape[:-1] + (CHUNKS, width))

    rate_chunk = rate[:, None, :] * steps
    y, gated, small = pl.pallas_call(
        functools.partial(scan_kernel, group, count),
        out_shape=(
            jax.ShapeDtypeStruct((3, steps, CHUNKS, width), f32),
            jax.ShapeDtypeStruct((steps, CHUNKS, width), f32),
            jax.ShapeDtypeStruct(((21 + modes + 7) // 8 * 8 + 8, width), f32),
        ),
        in_specs=[VMEM] * 10,
        out_specs=(VMEM,) * 3,
        scratch_shapes=[
            pltpu.VMEM((3, steps, CHUNKS, width), f32),
            pltpu.VMEM((steps, CHUNKS, width), f32),
            pltpu.VMEM((steps, CHUNKS, width), f32),
            pltpu.VMEM((3, steps + HALO, CHUNKS, width), f32),
            pltpu.VMEM((modes, CHUNKS, width), f32),
            pltpu.VMEM((modes, CHUNKS, width), f32),
            pltpu.VMEM((count, 2, modes, width), f32),
            pltpu.VMEM((3, HALO, width), f32),
            pltpu.VMEM((3, HALO, width), f32),
            DMA((count,)), DMA((count,)), DMA((1,)), DMA((1,)),
        ],
        compiler_params=params(1),
        name="scan",
    )(
        extended,
        upstream,
        spread(taps),
        spread(jnp.exp(-rate)),
        spread(coef),
        spread(jnp.exp(-rate * steps)),
        jnp.exp(-rate * span_tokens),
        jnp.exp(-rate_chunk * places),
        jnp.exp(-rate_chunk * (CHUNKS - 1.0 - places)),
        norm,
    )

    gated = jnp.swapaxes(gated, 0, 1).reshape(span_tokens, width).astype(bf16)
    partial = lax.dot_general(
        gated, out_rows, (((0,), (0,)), ((), ())), preferred_element_type=f32
    ).astype(bf16)
    y = jnp.swapaxes(y.astype(bf16), 1, 2).reshape(3, group, tokens, width)
    weight_grad, yo, so = pl.pallas_call(
        functools.partial(exchange_kernel, group, count, rows_dp),
        out_shape=(
            jax.ShapeDtypeStruct((own_rows, columns), f32),
            jax.ShapeDtypeStruct((group, 3, tokens, width), bf16),
            jax.ShapeDtypeStruct((group,) + small.shape, f32),
        ),
        in_specs=[VMEM] * 3,
        out_specs=(VMEM,) * 3,
        scratch_shapes=[
            pltpu.VMEM((count, own_rows, columns), bf16),
            pltpu.VMEM((rows_dp, own_rows, columns), bf16),
            pltpu.VMEM((count * rows_dp,) + small.shape, f32),
            DMA((count,)), DMA((count,)), DMA((group,)), DMA((group,)),
            DMA((count * rows_dp,)), DMA((count * rows_dp,)),
            DMA((group,)), DMA((group,)), DMA((rows_dp,)), DMA((rows_dp,)), DMA((1,)),
        ],
        compiler_params=params(2),
        name="exchange",
    )(partial.reshape(count, own_rows, columns), jnp.swapaxes(y, 0, 1), small)

    def joined(v):
        v = v.reshape(v.shape[:-1] + (count, own_rows))
        v = jnp.moveaxis(v, 0, -2)
        return v.reshape(v.shape[:-3] + (channels,))

    grads = joined(yo)
    sums = joined(so)
    taps_grad = jnp.swapaxes(sums[:21].reshape(3, 7, channels), 1, 2)
    residue_grad = sums[21 : 21 + modes].T
    return (grads[0][None], grads[1][None], grads[2][None], weight_grad, taps_grad, residue_grad)


def solution(mesh):
    placed = (
        P("dp", "ctx", None),
        P("dp", "ctx", None),
        P("dp", "ctx", None),
        P("dp", "ctx", None),
        P("ctx", None),
        P(),
        P(),
        P(),
    )
    return jax.shard_map(
        shards,
        mesh=mesh,
        in_specs=placed,
        out_specs=(
            P("dp", "ctx", None),
            P("dp", "ctx", None),
            P("dp", "ctx", None),
            P("ctx", None),
            P(),
            P(),
        ),
        check_vma=False,
    )
```

```python
import functools
import math

import jax
import jax.numpy as jnp
from jax import lax
from jax.experimental import pallas as pl
from jax.experimental.pallas import tpu as pltpu
from jax.sharding import PartitionSpec as P

LANES = 128
CHUNKS = 8
HALO = 8
PIECES = 4


def at_device(ctx, dp=None):
    return {"ctx": ctx} if dp is None else {"ctx": ctx, "dp": dp}


def greet_all(ctx_count, dp_count):
    barrier = pltpu.get_barrier_semaphore()
    me, row = lax.axis_index("ctx"), lax.axis_index("dp")
    for step in range(ctx_count):
        for other in range(dp_count):
            if step + other > 0:
                pl.semaphore_signal(
                    barrier,
                    inc=1,
                    device_id=at_device(
                        lax.rem(me + step, ctx_count),
                        None if dp_count == 1 else lax.rem(row + other, dp_count),
                    ),
                    device_id_type=pl.DeviceIdType.MESH,
                )
    pl.semaphore_wait(barrier, ctx_count * dp_count - 1)


def remote(src, dst, send, recv, ctx, dp=None):
    return pltpu.make_async_remote_copy(
        src_ref=src,
        dst_ref=dst,
        send_sem=send,
        recv_sem=recv,
        device_id=at_device(ctx, dp),
        device_id_type=pl.DeviceIdType.MESH,
    )


def gather_kernel(
    group, count, rows_dp, x_ref, go_ref, w_ref, xg_ref, gog_ref, wg_ref, halo_ref,
    xs, xr, gs, gr, fs, fr, ts, tr, ws, wr, ps, pr, hs, hr, own,
):
    me, row = lax.axis_index("ctx"), lax.axis_index("dp")
    mine, block = lax.rem(me, group), lax.div(me, group)
    tokens = go_ref.shape[0]
    part = w_ref.shape[1] // rows_dp
    columns = pl.ds(pl.multiple_of(row * part, part), part)
    pieces = gs.shape[0]
    tall = tokens // pieces
    across = lax.rem(mine + group // 2, group)
    twin = mine + 1 - 2 * lax.rem(mine, 2)
    home = block * group
    greet_all(group * count, rows_dp)
    weights = [
        remote(
            w_ref.at[:, columns],
            wg_ref.at[block, :, columns],
            ws.at[step],
            wr.at[step],
            lax.rem(block + step, count) * group + mine,
        )
        for step in range(1, count)
    ]
    swaps = []
    for step in range(1, count):
        held = wg_ref.at[lax.rem(block + count - step, count), :, columns]
        for other in range(1, rows_dp):
            at = step * rows_dp + other
            to = lax.rem(row + other, rows_dp)
            swaps.append((step, remote(held, held, ps.at[at], pr.at[at], me, to)))
    over, passed = [], []
    for k in range(pieces):
        tile = pl.ds(k * tall, tall)
        over.append(
            remote(go_ref.at[tile], gog_ref.at[mine, tile], gs.at[k], gr.at[k], home + across)
        )
        held = gog_ref.at[across, tile]
        passed.append(remote(held, held, fs.at[k], fr.at[k], home + twin))
    beside = remote(go_ref, gog_ref.at[mine], ts.at[0], tr.at[0], home + twin)
    streams = []
    for step in range(1, group):
        there = lax.rem(mine + step, group)
        streams.append(
            remote(x_ref.at[there], xg_ref.at[mine], xs.at[step], xr.at[step], home + there)
        )
    for copy in weights + over + streams + [beside]:
        copy.start()

    def halo_copy(there):
        ahead = jnp.minimum(block + 1, count - 1)
        return remote(
            x_ref.at[there, :, pl.ds(tokens - 16, 16), :],
            halo_ref,
            hs.at[there],
            hr.at[0],
            ahead * group + there,
        )

    @pl.when((mine == group - 1) & (block < count - 1))
    def _():
        for there in range(group):
            halo_copy(there).start()

    locals_ = [
        pltpu.make_async_copy(x_ref.at[mine], xg_ref.at[mine], own.at[0]),
        pltpu.make_async_copy(go_ref, gog_ref.at[mine], own.at[1]),
        pltpu.make_async_copy(w_ref, wg_ref.at[block], own.at[2]),
    ]
    for copy in locals_:
        copy.start()

    @pl.when(block == 0)
    def _():
        halo_ref[...] = jnp.zeros_like(halo_ref)

    def relay(k):
        over[k].wait_recv()
        passed[k].start()

    for k in range(pieces // 2):
        relay(k)
    for step in range(1, count):
        weights[step - 1].wait_recv()
        for at, copy in swaps:
            if at == step:
                copy.start()
        if pieces // 2 + step - 1 < pieces:
            relay(pieces // 2 + step - 1)
    for k in range(pieces // 2 + count - 1, pieces):
        relay(k)
    for copy in weights + over:
        copy.wait_send()
    for copy in locals_ + streams + passed + [beside] + [copy for _, copy in swaps]:
        copy.wait()

    @pl.when((mine == group - 1) & (block < count - 1))
    def _():
        for there in range(group):
            halo_copy(there).wait_send()

    @pl.when(block > 0)
    def _():
        halo_copy(0).wait_recv()


def tree_sum(parts):
    parts = list(parts)
    while len(parts) > 1:
        parts = [
            parts[k] + parts[k + 1] if k + 1 < len(parts) else parts[k]
            for k in range(0, len(parts), 2)
        ]
    return parts[0]


def scan_kernel(
    group, count, x_ref, up_ref, taps_row, factor_row, coef_row, rate_row, norm_ref,
    y_ref, gated_ref, small_ref, taps_ref, factor_ref, coef_ref,
    shaped, mixed, gradf, gext, starts, bstarts, states, hsend, hrecv,
    ss, sr, hss, hsr,
):
    me = lax.axis_index("ctx")
    mine, block = lax.rem(me, group), lax.div(me, group)
    steps = up_ref.shape[0]
    width = up_ref.shape[2]
    modes = factor_ref.shape[0]
    greet_all(group * count, 1)
    for m in range(modes):
        factor_ref[m] = jnp.broadcast_to(factor_row[m : m + 1], (CHUNKS, width))
        coef_ref[m] = jnp.broadcast_to(coef_row[m : m + 1], (CHUNKS, width))
    for i in range(3):
        for j in range(7):
            taps_ref[i, j] = jnp.broadcast_to(taps_row[i, j : j + 1], (CHUNKS, width))
    row = lax.broadcasted_iota(jnp.int32, (CHUNKS, LANES), 0)
    spans = [slice(k, k + LANES) for k in range(0, width, LANES)]

    def down(v):
        return jnp.where(row > 0, pltpu.roll(v, 1, 0), 0.0)

    def up(v):
        return jnp.where(row < CHUNKS - 1, pltpu.roll(v, CHUNKS - 1, 0), 0.0)

    zeros = tuple(jnp.zeros((CHUNKS, LANES), jnp.float32) for _ in range(modes))
    for span in spans:

        def first(s, state):
            made = []
            for i in range(3):
                total = tree_sum(
                    [taps_ref[i, j, :, span] * x_ref[i, s + HALO - j, :, span] for j in range(7)]
                )
                shaped[i, s, :, span] = total
                made.append(total)
            value = made[1] * made[2]
            mixed[s, :, span] = value
            gradf[s, :, span] = up_ref[s, :, span] * made[0]
            return tuple(factor_ref[m, :, span] * state[m] + value for m in range(modes))

        ends = lax.fori_loop(0, steps, first, zeros)

        def first_back(k, state):
            value = gradf[steps - 1 - k, :, span]
            return tuple(factor_ref[m, :, span] * state[m] + value for m in range(modes))

        firsts = lax.fori_loop(0, steps, first_back, zeros)
        for m in range(modes):
            fs = jnp.broadcast_to(
                jnp.exp(-rate_row[m : m + 1, span] * float(steps)), (CHUNKS, LANES)
            )
            a = jnp.zeros((CHUNKS, LANES), jnp.float32)
            b = a
            for _ in range(CHUNKS - 1):
                a = down(fs * a + ends[m])
                b = up(fs * b + firsts[m])
            starts[m, :, span] = a
            bstarts[m, :, span] = b
            states[block, 0, m : m + 1, span] = (fs * a + ends[m])[CHUNKS - 1 :]
            states[block, 1, m : m + 1, span] = (fs * b + firsts[m])[:1]

    copies = [
        remote(
            states.at[block],
            states.at[block],
            ss.at[step],
            sr.at[step],
            lax.rem(block + step, count) * group + mine,
        )
        for step in range(1, count)
    ]
    for copy in copies:
        copy.start()
    for copy in copies:
        copy.wait()
    incoming = jnp.zeros((modes, width), jnp.float32)
    outgoing = incoming
    decay = jnp.exp(-rate_row[...] * float(steps * CHUNKS))
    place = row.astype(jnp.float32) * float(steps)
    for k in range(count):
        incoming = jnp.where(k < block, decay * incoming + states[k, 0], incoming)
        r = count - 1 - k
        outgoing = jnp.where(r > block, decay * outgoing + states[r, 1], outgoing)
    for span in spans:
        for m in range(modes):
            rate = rate_row[m : m + 1, span]
            starts[m, :, span] += jnp.exp(-rate * place) * incoming[m : m + 1, span]
            far = float(steps * (CHUNKS - 1)) - place
            bstarts[m, :, span] += jnp.exp(-rate * far) * outgoing[m : m + 1, span]

    for span in spans:

        def second(s, state):
            value = mixed[s, :, span]
            new = tuple(factor_ref[m, :, span] * state[m] + value for m in range(modes))
            filtered = tree_sum([coef_ref[m, :, span] * new[m] for m in range(modes)])
            gated_ref[s, :, span] = shaped[0, s, :, span] * filtered
            gext[0, s, :, span] = up_ref[s, :, span] * filtered
            return new

        lax.fori_loop(0, steps, second, tuple(starts[m, :, span] for m in range(modes)))

        def second_back(k, carry):
            state, total = carry
            s = steps - 1 - k
            value = gradf[s, :, span]
            other = mixed[s, :, span]
            new = tuple(factor_ref[m, :, span] * state[m] + value for m in range(modes))
            total = tuple(total[m] + other * new[m] for m in range(modes))
            grad = tree_sum([coef_ref[m, :, span] * new[m] for m in range(modes)])
            gext[1, s, :, span] = grad * shaped[2, s, :, span]
            gext[2, s, :, span] = grad * shaped[1, s, :, span]
            return new, total

        _, total = lax.fori_loop(
            0, steps, second_back, (tuple(bstarts[m, :, span] for m in range(modes)), zeros)
        )
        for m in range(modes):
            small_ref[21 + m : 22 + m, span] = norm_ref[m : m + 1, span] * jnp.sum(
                total[m], axis=0, keepdims=True
            )
    small_ref[21 + modes :, :] = jnp.zeros((small_ref.shape[0] - 21 - modes, width), jnp.float32)

    for i in range(3):
        for s in range(HALO):
            hsend[i, s : s + 1, :] = gext[i, s, 0:1, :]
    ahead = remote(
        hsend, hrecv, hss.at[0], hsr.at[0], jnp.maximum(block - 1, 0) * group + mine
    )

    @pl.when(block > 0)
    def _():
        ahead.start()

    for span in spans:
        for i in range(3):

            def tap(s, sums):
                value = gext[i, s, :, span]
                return tuple(
                    sums[j] + value * x_ref[i, s + HALO - j, :, span] for j in range(7)
                )

            sums = lax.fori_loop(0, steps, tap, zeros[:7], unroll=2)
            for j in range(7):
                at = i * 7 + j
                small_ref[at : at + 1, span] = jnp.sum(sums[j], axis=0, keepdims=True)

    @pl.when(block == count - 1)
    def _():
        hrecv[...] = jnp.zeros_like(hrecv)

    @pl.when(block > 0)
    def _():
        ahead.wait_send()

    @pl.when(block < count - 1)
    def _():
        ahead.wait_recv()

    for span in spans:
        for i in range(3):
            for s in range(HALO):
                gext[i, steps + s, :, span] = jnp.where(
                    row < CHUNKS - 1,
                    pltpu.roll(gext[i, s, :, span], CHUNKS - 1, 0),
                    hrecv[i, s : s + 1, span],
                )

            def out(s, nothing):
                y_ref[i, s, :, span] = tree_sum(
                    [taps_ref[i, j, :, span] * gext[i, s + j, :, span] for j in range(7)]
                )
                return nothing

            lax.fori_loop(0, steps, out, 0, unroll=2)


def exchange_kernel(
    group, count, rows_dp, wp_ref, y_ref, small_ref, wg_ref, yo_ref, so_ref,
    wbuf, pair, qbuf, qsum, qz, qpair, sbuf,
    wsend, wrecv, ysend, yrecv, ssend, srecv, tsend, trecv, psend, precv,
    qsend, qrecv, zsend, zrecv, fsend, frecv, own,
):
    me, row = lax.axis_index("ctx"), lax.axis_index("dp")
    mine, block = lax.rem(me, group), lax.div(me, group)
    f32 = jnp.float32
    half = pair.shape[2]
    part = qpair.shape[2]
    tile = math.gcd(part, 512)
    greet_all(group * count, rows_dp)
    members = count * rows_dp
    slot = block * rows_dp + row
    smalls = []
    for step in range(1, members):
        there = lax.rem(slot + step, members)
        smalls.append(
            remote(
                small_ref,
                sbuf.at[slot],
                ssend.at[step],
                srecv.at[step],
                lax.div(there, rows_dp) * group + mine,
                lax.rem(there, rows_dp),
            )
        )
    weights, sums = [], []
    for step in range(1, count):
        there = lax.rem(block + step, count)
        to = there * group + mine
        weights.append(
            remote(
                wp_ref.at[there, :, pl.ds(0, half)], wbuf.at[step], wsend.at[step],
                wrecv.at[step], to,
            )
        )
        sums.append(remote(qsum.at[there], qz.at[step], zsend.at[step], zrecv.at[step], to))
    quarters, pairs, finals = [], [], []
    for step in range(1, rows_dp):
        to = lax.rem(row + step, rows_dp)
        columns = pl.ds(pl.multiple_of(half + to * part, part), part)
        quarters.append(
            remote(
                wp_ref.at[:, :, columns], qbuf.at[step], qsend.at[step], qrecv.at[step], me, to
            )
        )
        pairs.append(
            remote(pair.at[row], pair.at[row], psend.at[step], precv.at[step], me, to)
        )
        finals.append(
            remote(qpair.at[row], qpair.at[row], fsend.at[step], frecv.at[step], me, to)
        )
    outs, totals = [], []
    for step in range(1, group):
        there = lax.rem(mine + step, group)
        to = block * group + there
        outs.append(
            remote(y_ref.at[there], yo_ref.at[mine], ysend.at[step], yrecv.at[step], to)
        )
        totals.append(
            remote(so_ref.at[mine], so_ref.at[mine], tsend.at[step], trecv.at[step], to)
        )
    for copy in quarters + weights + outs + smalls:
        copy.start()
    keep = pltpu.make_async_copy(y_ref.at[mine], yo_ref.at[mine], own.at[0])
    keep.start()
    sbuf[slot] = small_ref[...]

    def each(width, body):
        def run(k, nothing):
            body(pl.multiple_of(k * tile, tile))
            return nothing

        lax.fori_loop(0, width // tile, run, 0)

    for copy in quarters:
        copy.wait()

    def add_rows(at):
        source = pl.ds(pl.multiple_of(half + row * part + at, tile), tile)
        at = pl.ds(at, tile)
        for k in range(count):
            value = wp_ref[k, :, source].astype(f32)
            for step in range(1, rows_dp):
                value = value + qbuf[step, k, :, at].astype(f32)
            qsum[k, :, at] = value.astype(qsum.dtype)

    each(part, add_rows)
    for copy in sums:
        copy.start()
    for copy in smalls:
        copy.wait()
    total = sbuf[0]
    for k in range(1, members):
        total = total + sbuf[k]
    so_ref[mine] = total
    for copy in totals:
        copy.start()
    for copy in weights:
        copy.wait()

    def add(at):
        at = pl.ds(at, tile)
        value = wp_ref[block, :, at].astype(f32)
        for step in range(1, count):
            value = value + wbuf[step, :, at].astype(f32)
        pair[row, :, at] = value.astype(pair.dtype)

    each(half, add)
    for copy in pairs:
        copy.start()
    for copy in sums:
        copy.wait()

    def add_blocks(at):
        at = pl.ds(at, tile)
        value = qsum[block, :, at].astype(f32)
        for step in range(1, count):
            value = value + qz[step, :, at].astype(f32)
        qpair[row, :, at] = value.astype(qpair.dtype)

    each(part, add_blocks)
    for copy in finals:
        copy.start()
    for copy in pairs:
        copy.wait()

    def finish(at):
        at = pl.ds(at, tile)
        value = pair[0, :, at].astype(f32)
        for other in range(1, rows_dp):
            value = value + pair[other, :, at].astype(f32)
        wg_ref[:, at] = value

    each(half, finish)
    for copy in finals:
        copy.wait()
    for other in range(rows_dp):

        def finish_part(at):
            to = pl.ds(pl.multiple_of(half + other * part + at, tile), tile)
            wg_ref[:, to] = qpair[other, :, pl.ds(at, tile)].astype(f32)

        each(part, finish_part)
    keep.wait()
    for copy in outs + totals:
        copy.wait()


VMEM = pl.BlockSpec(memory_space=pltpu.VMEM)
DMA = pltpu.SemaphoreType.DMA


def params(number):
    return pltpu.CompilerParams(
        collective_id=number, has_side_effects=True, vmem_limit_bytes=56 * 1024 * 1024
    )


def shards(
    query_proj, key_proj, value_proj, grad_out, out_weight, short_taps, residues, decay_rate
):
    devices, rows_dp = lax.axis_size("ctx"), lax.axis_size("dp")
    group = math.gcd(devices, 4)
    count = devices // group
    mine = lax.rem(lax.axis_index("ctx"), group)
    tokens, channels = query_proj.shape[1:]
    own_rows, columns = out_weight.shape
    width = count * own_rows
    modes = residues.shape[1]
    span_tokens = group * tokens
    steps = span_tokens // CHUNKS
    f32, bf16 = jnp.float32, jnp.bfloat16
    half = columns // 2
    part = half // rows_dp

    def parted(v):
        v = v.reshape(v.shape[:-1] + (count, group, own_rows))
        return jnp.moveaxis(v, -2, 0).reshape((group,) + v.shape[:-3] + (width,))

    def picked(v):
        return lax.dynamic_index_in_dim(parted(v), mine, 0, keepdims=False)

    streams = parted(jnp.stack([query_proj[0], key_proj[0], value_proj[0]]))
    xg, gog, wg, halo = pl.pallas_call(
        functools.partial(gather_kernel, group, count, rows_dp),
        out_shape=(
            jax.ShapeDtypeStruct((group, 3, tokens, width), bf16),
            jax.ShapeDtypeStruct((group, tokens, columns), bf16),
            jax.ShapeDtypeStruct((count, own_rows, columns), bf16),
            jax.ShapeDtypeStruct((3, 16, width), bf16),
        ),
        in_specs=[VMEM] * 3,
        out_specs=(VMEM,) * 4,
        scratch_shapes=[
            DMA((group,)), DMA((group,)), DMA((PIECES,)), DMA((PIECES,)),
            DMA((PIECES,)), DMA((PIECES,)), DMA((1,)), DMA((1,)),
            DMA((count,)), DMA((count,)), DMA((count * rows_dp,)), DMA((count * rows_dp,)),
            DMA((group,)), DMA((1,)), DMA((3,)),
        ],
        compiler_params=params(0),
        name="gather",
    )(streams, grad_out[0], out_weight)

    out_rows = gog.reshape(span_tokens, columns)
    upstream = lax.dot_general(
        out_rows,
        wg.reshape(width, columns),
        (((1,), (1,)), ((), ())),
        preferred_element_type=f32,
    )
    upstream = jnp.swapaxes(upstream.reshape(CHUNKS, steps, width), 0, 1)
    whole = jnp.swapaxes(xg, 0, 1).reshape(3, CHUNKS, steps, width)
    before = jnp.concatenate(
        [halo[:, None, 16 - HALO :], whole[:, :-1, steps - HALO :]], axis=1
    )
    extended = jnp.swapaxes(jnp.concatenate([before, whole], axis=2), 1, 2).astype(f32)

    taps = picked(jnp.swapaxes(short_taps, 1, 2))
    rate = picked(decay_rate.T)
    norm = jnp.sqrt(-jnp.expm1(-2.0 * rate))
    coef = picked(residues.T) * norm
    y, gated, small = pl.pallas_call(
        functools.partial(scan_kernel, group, count),
        out_shape=(
            jax.ShapeDtypeStruct((3, steps, CHUNKS, width), f32),
            jax.ShapeDtypeStruct((steps, CHUNKS, width), f32),
            jax.ShapeDtypeStruct(((21 + modes + 7) // 8 * 8 + 8, width), f32),
        ),
        in_specs=[VMEM] * 7,
        out_specs=(VMEM,) * 3,
        scratch_shapes=[
            pltpu.VMEM((3, 7, CHUNKS, width), f32),
            pltpu.VMEM((modes, CHUNKS, width), f32),
            pltpu.VMEM((modes, CHUNKS, width), f32),
            pltpu.VMEM((3, steps, CHUNKS, width), f32),
            pltpu.VMEM((steps, CHUNKS, width), f32),
            pltpu.VMEM((steps, CHUNKS, width), f32),
            pltpu.VMEM((3, steps + HALO, CHUNKS, width), f32),
            pltpu.VMEM((modes, CHUNKS, width), f32),
            pltpu.VMEM((modes, CHUNKS, width), f32),
            pltpu.VMEM((count, 2, modes, width), f32),
            pltpu.VMEM((3, HALO, width), f32),
            pltpu.VMEM((3, HALO, width), f32),
            DMA((count,)), DMA((count,)), DMA((1,)), DMA((1,)),
        ],
        compiler_params=params(1),
        name="scan",
    )(
        extended,
        upstream,
        taps,
        jnp.exp(-rate),
        coef,
        rate,
        norm,
    )

    gated = jnp.swapaxes(gated, 0, 1).reshape(span_tokens, width).astype(bf16)
    partial = lax.dot_general(
        gated, out_rows, (((0,), (0,)), ((), ())), preferred_element_type=f32
    ).astype(bf16)
    y = jnp.swapaxes(y.astype(bf16), 1, 2).reshape(3, group, tokens, width)
    weight_grad, yo, so = pl.pallas_call(
        functools.partial(exchange_kernel, group, count, rows_dp),
        out_shape=(
            jax.ShapeDtypeStruct((own_rows, columns), f32),
            jax.ShapeDtypeStruct((group, 3, tokens, width), bf16),
            jax.ShapeDtypeStruct((group,) + small.shape, f32),
        ),
        in_specs=[VMEM] * 3,
        out_specs=(VMEM,) * 3,
        scratch_shapes=[
            pltpu.VMEM((count, own_rows, half), bf16),
            pltpu.VMEM((rows_dp, own_rows, half), bf16),
            pltpu.VMEM((rows_dp, count, own_rows, part), bf16),
            pltpu.VMEM((count, own_rows, part), bf16),
            pltpu.VMEM((count, own_rows, part), bf16),
            pltpu.VMEM((rows_dp, own_rows, part), bf16),
            pltpu.VMEM((count * rows_dp,) + small.shape, f32),
            DMA((count,)), DMA((count,)), DMA((group,)), DMA((group,)),
            DMA((count * rows_dp,)), DMA((count * rows_dp,)),
            DMA((group,)), DMA((group,)), DMA((rows_dp,)), DMA((rows_dp,)),
            DMA((rows_dp,)), DMA((rows_dp,)), DMA((count,)), DMA((count,)),
            DMA((rows_dp,)), DMA((rows_dp,)), DMA((1,)),
        ],
        compiler_params=params(2),
        name="exchange",
    )(partial.reshape(count, own_rows, columns), jnp.swapaxes(y, 0, 1), small)

    def joined(v):
        v = v.reshape(v.shape[:-1] + (count, own_rows))
        v = jnp.moveaxis(v, 0, -2)
        return v.reshape(v.shape[:-3] + (channels,))

    grads = joined(yo)
    sums = joined(so)
    taps_grad = jnp.swapaxes(sums[:21].reshape(3, 7, channels), 1, 2)
    residue_grad = sums[21 : 21 + modes].T
    return (grads[0][None], grads[1][None], grads[2][None], weight_grad, taps_grad, residue_grad)


def solution(mesh):
    placed = (
        P("dp", "ctx", None),
        P("dp", "ctx", None),
        P("dp", "ctx", None),
        P("dp", "ctx", None),
        P("ctx", None),
        P(),
        P(),
        P(),
    )
    return jax.shard_map(
        shards,
        mesh=mesh,
        in_specs=placed,
        out_specs=(
            P("dp", "ctx", None),
            P("dp", "ctx", None),
            P("dp", "ctx", None),
            P("ctx", None),
            P(),
            P(),
        ),
        check_vma=False,
    )
```

```python
import functools
import math

import jax
import jax.numpy as jnp
from jax import lax
from jax.experimental import pallas as pl
from jax.experimental.pallas import tpu as pltpu
from jax.sharding import PartitionSpec as P

LANES = 128
CHUNKS = 8
HALO = 8
PIECES = 4


def at_device(ctx, dp=None):
    return {"ctx": ctx} if dp is None else {"ctx": ctx, "dp": dp}


def greet_all(ctx_count, dp_count):
    barrier = pltpu.get_barrier_semaphore()
    me, row = lax.axis_index("ctx"), lax.axis_index("dp")
    for step in range(ctx_count):
        for other in range(dp_count):
            if step + other > 0:
                pl.semaphore_signal(
                    barrier,
                    inc=1,
                    device_id=at_device(
                        lax.rem(me + step, ctx_count),
                        None if dp_count == 1 else lax.rem(row + other, dp_count),
                    ),
                    device_id_type=pl.DeviceIdType.MESH,
                )
    pl.semaphore_wait(barrier, ctx_count * dp_count - 1)


def remote(src, dst, send, recv, ctx, dp=None):
    return pltpu.make_async_remote_copy(
        src_ref=src,
        dst_ref=dst,
        send_sem=send,
        recv_sem=recv,
        device_id=at_device(ctx, dp),
        device_id_type=pl.DeviceIdType.MESH,
    )


def gather_kernel(
    group, count, rows_dp, x_ref, go_ref, w_ref, xg_ref, gog_ref, wg_ref, halo_ref,
    xs, xr, gs, gr, fs, fr, ts, tr, ws, wr, ps, pr, hs, hr, own,
):
    me, row = lax.axis_index("ctx"), lax.axis_index("dp")
    mine, block = lax.rem(me, group), lax.div(me, group)
    tokens = go_ref.shape[0]
    part = w_ref.shape[1] // rows_dp
    columns = pl.ds(pl.multiple_of(row * part, part), part)
    pieces = gs.shape[0]
    tall = tokens // pieces
    across = lax.rem(mine + group // 2, group)
    twin = mine + 1 - 2 * lax.rem(mine, 2)
    home = block * group
    greet_all(group * count, rows_dp)
    weights = [
        remote(
            w_ref.at[:, columns],
            wg_ref.at[block, :, columns],
            ws.at[step],
            wr.at[step],
            lax.rem(block + step, count) * group + mine,
        )
        for step in range(1, count)
    ]
    swaps = []
    for step in range(1, count):
        held = wg_ref.at[lax.rem(block + count - step, count), :, columns]
        for other in range(1, rows_dp):
            at = step * rows_dp + other
            to = lax.rem(row + other, rows_dp)
            swaps.append((step, remote(held, held, ps.at[at], pr.at[at], me, to)))
    over, passed = [], []
    for k in range(pieces):
        tile = pl.ds(k * tall, tall)
        over.append(
            remote(go_ref.at[tile], gog_ref.at[mine, tile], gs.at[k], gr.at[k], home + across)
        )
        held = gog_ref.at[across, tile]
        passed.append(remote(held, held, fs.at[k], fr.at[k], home + twin))
    beside = remote(go_ref, gog_ref.at[mine], ts.at[0], tr.at[0], home + twin)
    streams = []
    for step in range(1, group):
        there = lax.rem(mine + step, group)
        streams.append(
            remote(x_ref.at[there], xg_ref.at[mine], xs.at[step], xr.at[step], home + there)
        )
    for copy in weights + over + streams + [beside]:
        copy.start()

    def halo_copy(there):
        ahead = jnp.minimum(block + 1, count - 1)
        return remote(
            x_ref.at[there, :, pl.ds(tokens - 16, 16), :],
            halo_ref,
            hs.at[there],
            hr.at[0],
            ahead * group + there,
        )

    @pl.when((mine == group - 1) & (block < count - 1))
    def _():
        for there in range(group):
            halo_copy(there).start()

    locals_ = [
        pltpu.make_async_copy(x_ref.at[mine], xg_ref.at[mine], own.at[0]),
        pltpu.make_async_copy(go_ref, gog_ref.at[mine], own.at[1]),
        pltpu.make_async_copy(w_ref, wg_ref.at[block], own.at[2]),
    ]
    for copy in locals_:
        copy.start()

    @pl.when(block == 0)
    def _():
        halo_ref[...] = jnp.zeros_like(halo_ref)

    def relay(k):
        over[k].wait_recv()
        passed[k].start()

    for k in range(pieces // 2):
        relay(k)
    for step in range(1, count):
        weights[step - 1].wait_recv()
        for at, copy in swaps:
            if at == step:
                copy.start()
        if pieces // 2 + step - 1 < pieces:
            relay(pieces // 2 + step - 1)
    for k in range(pieces // 2 + count - 1, pieces):
        relay(k)
    for copy in weights + over:
        copy.wait_send()
    for copy in locals_ + streams + passed + [beside] + [copy for _, copy in swaps]:
        copy.wait()

    @pl.when((mine == group - 1) & (block < count - 1))
    def _():
        for there in range(group):
            halo_copy(there).wait_send()

    @pl.when(block > 0)
    def _():
        halo_copy(0).wait_recv()


def tree_sum(parts):
    parts = list(parts)
    while len(parts) > 1:
        parts = [
            parts[k] + parts[k + 1] if k + 1 < len(parts) else parts[k]
            for k in range(0, len(parts), 2)
        ]
    return parts[0]


def scan_kernel(
    group, count, rows_dp, x_ref, up_ref, taps_row, factor_row, coef_row, rate_row, norm_ref,
    go_ref, wg_ref, yo_ref, so_ref, taps_ref, factor_ref, coef_ref,
    shaped, mixed, gradf, gext, starts, bstarts, states, hsend, hrecv,
    gated_ref, gated_t, small_ref, wp_ref, y_ref,
    wbuf, pair, qbuf, qsum, qz, qpair, sbuf,
    ss, sr, hss, hsr, wsend, wrecv, ysend, yrecv, ssend, srecv, tsend, trecv, psend, precv,
    qsend, qrecv, zsend, zrecv, fsend, frecv, own,
):
    me = lax.axis_index("ctx")
    line = lax.axis_index("dp")
    mine, block = lax.rem(me, group), lax.div(me, group)
    steps = up_ref.shape[0]
    width = up_ref.shape[2]
    modes = factor_ref.shape[0]
    greet_all(group * count, rows_dp)
    for m in range(modes):
        factor_ref[m] = jnp.broadcast_to(factor_row[m : m + 1], (CHUNKS, width))
        coef_ref[m] = jnp.broadcast_to(coef_row[m : m + 1], (CHUNKS, width))
    for i in range(3):
        for j in range(7):
            taps_ref[i, j] = jnp.broadcast_to(taps_row[i, j : j + 1], (CHUNKS, width))
    row = lax.broadcasted_iota(jnp.int32, (CHUNKS, LANES), 0)
    spans = [slice(k, k + LANES) for k in range(0, width, LANES)]

    def down(v):
        return jnp.where(row > 0, pltpu.roll(v, 1, 0), 0.0)

    def up(v):
        return jnp.where(row < CHUNKS - 1, pltpu.roll(v, CHUNKS - 1, 0), 0.0)

    zeros = tuple(jnp.zeros((CHUNKS, LANES), jnp.float32) for _ in range(modes))
    for span in spans:

        def first(s, state):
            made = []
            for i in range(3):
                total = tree_sum(
                    [taps_ref[i, j, :, span] * x_ref[i, s + HALO - j, :, span] for j in range(7)]
                )
                shaped[i, s, :, span] = total
                made.append(total)
            value = made[1] * made[2]
            mixed[s, :, span] = value
            gradf[s, :, span] = up_ref[s, :, span] * made[0]
            return tuple(factor_ref[m, :, span] * state[m] + value for m in range(modes))

        ends = lax.fori_loop(0, steps, first, zeros)

        def first_back(k, state):
            value = gradf[steps - 1 - k, :, span]
            return tuple(factor_ref[m, :, span] * state[m] + value for m in range(modes))

        firsts = lax.fori_loop(0, steps, first_back, zeros)
        for m in range(modes):
            fs = jnp.broadcast_to(
                jnp.exp(-rate_row[m : m + 1, span] * float(steps)), (CHUNKS, LANES)
            )
            a = jnp.zeros((CHUNKS, LANES), jnp.float32)
            b = a
            for _ in range(CHUNKS - 1):
                a = down(fs * a + ends[m])
                b = up(fs * b + firsts[m])
            starts[m, :, span] = a
            bstarts[m, :, span] = b
            states[block, 0, m : m + 1, span] = (fs * a + ends[m])[CHUNKS - 1 :]
            states[block, 1, m : m + 1, span] = (fs * b + firsts[m])[:1]

    copies = [
        remote(
            states.at[block],
            states.at[block],
            ss.at[step],
            sr.at[step],
            lax.rem(block + step, count) * group + mine,
        )
        for step in range(1, count)
    ]
    for copy in copies:
        copy.start()
    for copy in copies:
        copy.wait()
    incoming = jnp.zeros((modes, width), jnp.float32)
    outgoing = incoming
    decay = jnp.exp(-rate_row[...] * float(steps * CHUNKS))
    place = row.astype(jnp.float32) * float(steps)
    for k in range(count):
        incoming = jnp.where(k < block, decay * incoming + states[k, 0], incoming)
        r = count - 1 - k
        outgoing = jnp.where(r > block, decay * outgoing + states[r, 1], outgoing)
    for span in spans:
        for m in range(modes):
            rate = rate_row[m : m + 1, span]
            starts[m, :, span] += jnp.exp(-rate * place) * incoming[m : m + 1, span]
            far = float(steps * (CHUNKS - 1)) - place
            bstarts[m, :, span] += jnp.exp(-rate * far) * outgoing[m : m + 1, span]

    for span in spans:

        def second(s, state):
            value = mixed[s, :, span]
            new = tuple(factor_ref[m, :, span] * state[m] + value for m in range(modes))
            filtered = tree_sum([coef_ref[m, :, span] * new[m] for m in range(modes)])
            gated_ref[s, :, span] = shaped[0, s, :, span] * filtered
            gext[0, s, :, span] = up_ref[s, :, span] * filtered
            return new

        lax.fori_loop(0, steps, second, tuple(starts[m, :, span] for m in range(modes)))
        gated_t[span, :] = jnp.swapaxes(
            jnp.swapaxes(gated_ref[:, :, span], 0, 1).reshape(steps * CHUNKS, LANES), 0, 1
        ).astype(gated_t.dtype)

    f32 = jnp.float32
    half = pair.shape[2]
    part = qpair.shape[2]
    tile = math.gcd(part, 512)
    members = count * rows_dp
    slot = block * rows_dp + line
    smalls = []
    for step in range(1, members):
        there = lax.rem(slot + step, members)
        smalls.append(
            remote(
                small_ref,
                sbuf.at[slot],
                ssend.at[step],
                srecv.at[step],
                lax.div(there, rows_dp) * group + mine,
                lax.rem(there, rows_dp),
            )
        )
    weights, sums = [], []
    for step in range(1, count):
        there = lax.rem(block + step, count)
        to = there * group + mine
        weights.append(
            remote(
                wp_ref.at[there, :, pl.ds(0, half)], wbuf.at[step], wsend.at[step],
                wrecv.at[step], to,
            )
        )
        sums.append(remote(qsum.at[there], qz.at[step], zsend.at[step], zrecv.at[step], to))
    quarters, pairs, finals = [], [], []
    for step in range(1, rows_dp):
        to = lax.rem(line + step, rows_dp)
        columns = pl.ds(pl.multiple_of(half + to * part, part), part)
        quarters.append(
            remote(
                wp_ref.at[:, :, columns], qbuf.at[step], qsend.at[step], qrecv.at[step], me, to
            )
        )
        pairs.append(
            remote(pair.at[line], pair.at[line], psend.at[step], precv.at[step], me, to)
        )
        finals.append(
            remote(qpair.at[line], qpair.at[line], fsend.at[step], frecv.at[step], me, to)
        )
    outs, totals = [], []
    for step in range(1, group):
        there = lax.rem(mine + step, group)
        to = block * group + there
        outs.append(
            remote(y_ref.at[there], yo_ref.at[mine], ysend.at[step], yrecv.at[step], to)
        )
        totals.append(
            remote(so_ref.at[mine], so_ref.at[mine], tsend.at[step], trecv.at[step], to)
        )
    def each(width, body):
        def run(k, nothing):
            body(pl.multiple_of(k * tile, tile))
            return nothing

        lax.fori_loop(0, width // tile, run, 0)


    own_rows = wp_ref.shape[1]

    def product(at):
        at = pl.ds(at, tile)
        value = jnp.dot(gated_t[...], go_ref[:, at], preferred_element_type=f32)
        value = value.astype(wp_ref.dtype)
        for k in range(count):
            wp_ref[k, :, at] = value[k * own_rows : (k + 1) * own_rows]

    each(half, lambda at: product(pl.multiple_of(half + at, tile)))
    for copy in quarters:
        copy.start()
    each(half, product)
    for copy in weights:
        copy.start()

    for span in spans:

        def second_back(k, carry):
            state, total = carry
            s = steps - 1 - k
            value = gradf[s, :, span]
            other = mixed[s, :, span]
            new = tuple(factor_ref[m, :, span] * state[m] + value for m in range(modes))
            total = tuple(total[m] + other * new[m] for m in range(modes))
            grad = tree_sum([coef_ref[m, :, span] * new[m] for m in range(modes)])
            gext[1, s, :, span] = grad * shaped[2, s, :, span]
            gext[2, s, :, span] = grad * shaped[1, s, :, span]
            return new, total

        _, total = lax.fori_loop(
            0, steps, second_back, (tuple(bstarts[m, :, span] for m in range(modes)), zeros)
        )
        for m in range(modes):
            small_ref[21 + m : 22 + m, span] = norm_ref[m : m + 1, span] * jnp.sum(
                total[m], axis=0, keepdims=True
            )
    if small_ref.shape[0] > 21 + modes:
        small_ref[21 + modes :, :] = jnp.zeros(
            (small_ref.shape[0] - 21 - modes, width), jnp.float32
        )

    for i in range(3):
        for s in range(HALO):
            hsend[i, s : s + 1, :] = gext[i, s, 0:1, :]
    ahead = remote(
        hsend, hrecv, hss.at[0], hsr.at[0], jnp.maximum(block - 1, 0) * group + mine
    )

    @pl.when(block > 0)
    def _():
        ahead.start()

    for span in spans:
        for i in range(3):

            def tap(s, sums):
                value = gext[i, s, :, span]
                return tuple(
                    sums[j] + value * x_ref[i, s + HALO - j, :, span] for j in range(7)
                )

            tapped = lax.fori_loop(0, steps, tap, zeros[:7], unroll=2)
            for j in range(7):
                at = i * 7 + j
                small_ref[at : at + 1, span] = jnp.sum(tapped[j], axis=0, keepdims=True)

    sbuf[slot] = small_ref[...]
    for copy in smalls:
        copy.start()
    for copy in quarters:
        copy.wait()

    def add_rows(at):
        source = pl.ds(pl.multiple_of(half + line * part + at, tile), tile)
        at = pl.ds(at, tile)
        for k in range(count):
            value = wp_ref[k, :, source].astype(f32)
            for step in range(1, rows_dp):
                value = value + qbuf[step, k, :, at].astype(f32)
            qsum[k, :, at] = value.astype(qsum.dtype)

    each(part, add_rows)
    for copy in sums:
        copy.start()

    @pl.when(block == count - 1)
    def _():
        hrecv[...] = jnp.zeros_like(hrecv)

    @pl.when(block > 0)
    def _():
        ahead.wait_send()

    @pl.when(block < count - 1)
    def _():
        ahead.wait_recv()

    for span in spans:
        for i in range(3):
            for s in range(HALO):
                gext[i, steps + s, :, span] = jnp.where(
                    row < CHUNKS - 1,
                    pltpu.roll(gext[i, s, :, span], CHUNKS - 1, 0),
                    hrecv[i, s : s + 1, span],
                )

            def out(s, nothing):
                shaped[i, s, :, span] = tree_sum(
                    [taps_ref[i, j, :, span] * gext[i, s + j, :, span] for j in range(7)]
                )
                return nothing

            lax.fori_loop(0, steps, out, 0, unroll=2)
            value = jnp.swapaxes(shaped[i, :, :, span], 0, 1).astype(y_ref.dtype)
            y_ref[:, i, :, span] = value.reshape(group, y_ref.shape[2], LANES)

    for copy in outs:
        copy.start()
    keep = pltpu.make_async_copy(y_ref.at[mine], yo_ref.at[mine], own.at[0])
    keep.start()
    for copy in smalls:
        copy.wait()
    total = sbuf[0]
    for k in range(1, members):
        total = total + sbuf[k]
    so_ref[mine] = total
    for copy in totals:
        copy.start()
    for copy in weights:
        copy.wait()

    def add(at):
        at = pl.ds(at, tile)
        value = wp_ref[block, :, at].astype(f32)
        for step in range(1, count):
            value = value + wbuf[step, :, at].astype(f32)
        pair[line, :, at] = value.astype(pair.dtype)

    each(half, add)
    for copy in pairs:
        copy.start()
    for copy in sums:
        copy.wait()

    def add_blocks(at):
        at = pl.ds(at, tile)
        value = qsum[block, :, at].astype(f32)
        for step in range(1, count):
            value = value + qz[step, :, at].astype(f32)
        qpair[line, :, at] = value.astype(qpair.dtype)

    each(part, add_blocks)
    for copy in finals:
        copy.start()
    for copy in pairs:
        copy.wait()

    def finish(at):
        at = pl.ds(at, tile)
        value = pair[0, :, at].astype(f32)
        for other in range(1, rows_dp):
            value = value + pair[other, :, at].astype(f32)
        wg_ref[:, at] = value

    each(half, finish)
    for copy in finals:
        copy.wait()
    for other in range(rows_dp):

        def finish_part(at):
            to = pl.ds(pl.multiple_of(half + other * part + at, tile), tile)
            wg_ref[:, to] = qpair[other, :, pl.ds(at, tile)].astype(f32)

        each(part, finish_part)
    keep.wait()
    for copy in outs + totals:
        copy.wait()


VMEM = pl.BlockSpec(memory_space=pltpu.VMEM)
DMA = pltpu.SemaphoreType.DMA


def params(number):
    return pltpu.CompilerParams(
        collective_id=number, has_side_effects=True, vmem_limit_bytes=56 * 1024 * 1024
    )


def shards(
    query_proj, key_proj, value_proj, grad_out, out_weight, short_taps, residues, decay_rate
):
    devices, rows_dp = lax.axis_size("ctx"), lax.axis_size("dp")
    group = math.gcd(devices, 4)
    count = devices // group
    mine = lax.rem(lax.axis_index("ctx"), group)
    tokens, channels = query_proj.shape[1:]
    own_rows, columns = out_weight.shape
    width = count * own_rows
    modes = residues.shape[1]
    span_tokens = group * tokens
    steps = span_tokens // CHUNKS
    f32, bf16 = jnp.float32, jnp.bfloat16
    half = columns // 2
    part = half // rows_dp

    def parted(v):
        v = v.reshape(v.shape[:-1] + (count, group, own_rows))
        return jnp.moveaxis(v, -2, 0).reshape((group,) + v.shape[:-3] + (width,))

    def picked(v):
        return lax.dynamic_index_in_dim(parted(v), mine, 0, keepdims=False)

    streams = parted(jnp.stack([query_proj[0], key_proj[0], value_proj[0]]))
    xg, gog, wg, halo = pl.pallas_call(
        functools.partial(gather_kernel, group, count, rows_dp),
        out_shape=(
            jax.ShapeDtypeStruct((group, 3, tokens, width), bf16),
            jax.ShapeDtypeStruct((group, tokens, columns), bf16),
            jax.ShapeDtypeStruct((count, own_rows, columns), bf16),
            jax.ShapeDtypeStruct((3, 16, width), bf16),
        ),
        in_specs=[VMEM] * 3,
        out_specs=(VMEM,) * 4,
        scratch_shapes=[
            DMA((group,)), DMA((group,)), DMA((PIECES,)), DMA((PIECES,)),
            DMA((PIECES,)), DMA((PIECES,)), DMA((1,)), DMA((1,)),
            DMA((count,)), DMA((count,)), DMA((count * rows_dp,)), DMA((count * rows_dp,)),
            DMA((group,)), DMA((1,)), DMA((3,)),
        ],
        compiler_params=params(0),
        name="gather",
    )(streams, grad_out[0], out_weight)

    out_rows = gog.reshape(span_tokens, columns)
    upstream = lax.dot_general(
        out_rows,
        wg.reshape(width, columns),
        (((1,), (1,)), ((), ())),
        preferred_element_type=f32,
    )
    upstream = jnp.swapaxes(upstream.reshape(CHUNKS, steps, width), 0, 1)
    whole = jnp.swapaxes(xg, 0, 1).reshape(3, CHUNKS, steps, width)
    before = jnp.concatenate(
        [halo[:, None, 16 - HALO :], whole[:, :-1, steps - HALO :]], axis=1
    )
    extended = jnp.swapaxes(jnp.concatenate([before, whole], axis=2), 1, 2).astype(f32)

    taps = picked(jnp.swapaxes(short_taps, 1, 2))
    rate = picked(decay_rate.T)
    norm = jnp.sqrt(-jnp.expm1(-2.0 * rate))
    coef = picked(residues.T) * norm
    tall = (21 + modes + 7) // 8 * 8
    small = (tall, width)
    weight_grad, yo, so = pl.pallas_call(
        functools.partial(scan_kernel, group, count, rows_dp),
        out_shape=(
            jax.ShapeDtypeStruct((own_rows, columns), f32),
            jax.ShapeDtypeStruct((group, 3, tokens, width), bf16),
            jax.ShapeDtypeStruct((group,) + small, f32),
        ),
        in_specs=[VMEM] * 8,
        out_specs=(VMEM,) * 3,
        scratch_shapes=[
            pltpu.VMEM((3, 7, CHUNKS, width), f32),
            pltpu.VMEM((modes, CHUNKS, width), f32),
            pltpu.VMEM((modes, CHUNKS, width), f32),
            pltpu.VMEM((3, steps, CHUNKS, width), f32),
            pltpu.VMEM((steps, CHUNKS, width), f32),
            pltpu.VMEM((steps, CHUNKS, width), f32),
            pltpu.VMEM((3, steps + HALO, CHUNKS, width), f32),
            pltpu.VMEM((modes, CHUNKS, width), f32),
            pltpu.VMEM((modes, CHUNKS, width), f32),
            pltpu.VMEM((count, 2, modes, width), f32),
            pltpu.VMEM((3, HALO, width), f32),
            pltpu.VMEM((3, HALO, width), f32),
            pltpu.VMEM((steps, CHUNKS, width), f32),
            pltpu.VMEM((width, span_tokens), bf16),
            pltpu.VMEM(small, f32),
            pltpu.VMEM((count, own_rows, columns), bf16),
            pltpu.VMEM((group, 3, tokens, width), bf16),
            pltpu.VMEM((count, own_rows, half), bf16),
            pltpu.VMEM((rows_dp, own_rows, half), bf16),
            pltpu.VMEM((rows_dp, count, own_rows, part), bf16),
            pltpu.VMEM((count, own_rows, part), bf16),
            pltpu.VMEM((count, own_rows, part), bf16),
            pltpu.VMEM((rows_dp, own_rows, part), bf16),
            pltpu.VMEM((count * rows_dp,) + small, f32),
            DMA((count,)), DMA((count,)), DMA((1,)), DMA((1,)),
            DMA((count,)), DMA((count,)), DMA((group,)), DMA((group,)),
            DMA((count * rows_dp,)), DMA((count * rows_dp,)),
            DMA((group,)), DMA((group,)), DMA((rows_dp,)), DMA((rows_dp,)),
            DMA((rows_dp,)), DMA((rows_dp,)), DMA((count,)), DMA((count,)),
            DMA((rows_dp,)), DMA((rows_dp,)), DMA((1,)),
        ],
        compiler_params=params(1),
        name="scan",
    )(extended, upstream, taps, jnp.exp(-rate), coef, rate, norm, out_rows)

    def joined(v):
        v = v.reshape(v.shape[:-1] + (count, own_rows))
        v = jnp.moveaxis(v, 0, -2)
        return v.reshape(v.shape[:-3] + (channels,))

    grads = joined(yo)
    sums = joined(so)
    taps_grad = jnp.swapaxes(sums[:21].reshape(3, 7, channels), 1, 2)
    residue_grad = sums[21 : 21 + modes].T
    return (grads[0][None], grads[1][None], grads[2][None], weight_grad, taps_grad, residue_grad)


def solution(mesh):
    placed = (
        P("dp", "ctx", None),
        P("dp", "ctx", None),
        P("dp", "ctx", None),
        P("dp", "ctx", None),
        P("ctx", None),
        P(),
        P(),
        P(),
    )
    return jax.shard_map(
        shards,
        mesh=mesh,
        in_specs=placed,
        out_specs=(
            P("dp", "ctx", None),
            P("dp", "ctx", None),
            P("dp", "ctx", None),
            P("ctx", None),
            P(),
            P(),
        ),
        check_vma=False,
    )
```

```python
import functools
import math

import jax
import jax.numpy as jnp
from jax import lax
from jax.experimental import pallas as pl
from jax.experimental.pallas import tpu as pltpu
from jax.sharding import PartitionSpec as P

LANES = 128
CHUNKS = 8
HALO = 8
PIECES = 4
ROUNDS = 3


def at_device(ctx, dp=None):
    return {"ctx": ctx} if dp is None else {"ctx": ctx, "dp": dp}


def greet_all(ctx_count, dp_count):
    barrier = pltpu.get_barrier_semaphore()
    me, row = lax.axis_index("ctx"), lax.axis_index("dp")
    for step in range(ctx_count):
        for other in range(dp_count):
            if step + other > 0:
                pl.semaphore_signal(
                    barrier,
                    inc=1,
                    device_id=at_device(
                        lax.rem(me + step, ctx_count),
                        None if dp_count == 1 else lax.rem(row + other, dp_count),
                    ),
                    device_id_type=pl.DeviceIdType.MESH,
                )
    pl.semaphore_wait(barrier, ctx_count * dp_count - 1)


def remote(src, dst, send, recv, ctx, dp=None):
    return pltpu.make_async_remote_copy(
        src_ref=src,
        dst_ref=dst,
        send_sem=send,
        recv_sem=recv,
        device_id=at_device(ctx, dp),
        device_id_type=pl.DeviceIdType.MESH,
    )


def gather_kernel(
    group, count, rows_dp, x_ref, go_ref, w_ref, xg_ref, gog_ref, wg_ref, halo_ref,
    xs, xr, gs, gr, fs, fr, ts, tr, ws, wr, ps, pr, hs, hr, own,
):
    me, row = lax.axis_index("ctx"), lax.axis_index("dp")
    mine, block = lax.rem(me, group), lax.div(me, group)
    tokens = go_ref.shape[0]
    part = w_ref.shape[1] // rows_dp
    columns = pl.ds(pl.multiple_of(row * part, part), part)
    pieces = gs.shape[0]
    tall = tokens // pieces
    across = lax.rem(mine + group // 2, group)
    twin = mine + 1 - 2 * lax.rem(mine, 2)
    home = block * group
    greet_all(group * count, rows_dp)
    weights = [
        remote(
            w_ref.at[:, columns],
            wg_ref.at[block, :, columns],
            ws.at[step],
            wr.at[step],
            lax.rem(block + step, count) * group + mine,
        )
        for step in range(1, count)
    ]
    swaps = []
    for step in range(1, count):
        held = wg_ref.at[lax.rem(block + count - step, count), :, columns]
        for other in range(1, rows_dp):
            at = step * rows_dp + other
            to = lax.rem(row + other, rows_dp)
            swaps.append((step, remote(held, held, ps.at[at], pr.at[at], me, to)))
    over, passed = [], []
    for k in range(pieces):
        tile = pl.ds(k * tall, tall)
        over.append(
            remote(go_ref.at[tile], gog_ref.at[mine, tile], gs.at[k], gr.at[k], home + across)
        )
        held = gog_ref.at[across, tile]
        passed.append(remote(held, held, fs.at[k], fr.at[k], home + twin))
    beside = remote(go_ref, gog_ref.at[mine], ts.at[0], tr.at[0], home + twin)
    streams = []
    for step in range(1, group):
        there = lax.rem(mine + step, group)
        streams.append(
            remote(x_ref.at[there], xg_ref.at[mine], xs.at[step], xr.at[step], home + there)
        )
    for copy in weights + over + streams + [beside]:
        copy.start()

    def halo_copy(there):
        ahead = jnp.minimum(block + 1, count - 1)
        return remote(
            x_ref.at[there, :, pl.ds(tokens - 16, 16), :],
            halo_ref,
            hs.at[there],
            hr.at[0],
            ahead * group + there,
        )

    @pl.when((mine == group - 1) & (block < count - 1))
    def _():
        for there in range(group):
            halo_copy(there).start()

    locals_ = [
        pltpu.make_async_copy(x_ref.at[mine], xg_ref.at[mine], own.at[0]),
        pltpu.make_async_copy(go_ref, gog_ref.at[mine], own.at[1]),
        pltpu.make_async_copy(w_ref, wg_ref.at[block], own.at[2]),
    ]
    for copy in locals_:
        copy.start()

    @pl.when(block == 0)
    def _():
        halo_ref[...] = jnp.zeros_like(halo_ref)

    def relay(k):
        over[k].wait_recv()
        passed[k].start()

    for k in range(pieces // 2):
        relay(k)
    for step in range(1, count):
        weights[step - 1].wait_recv()
        for at, copy in swaps:
            if at == step:
                copy.start()
        if pieces // 2 + step - 1 < pieces:
            relay(pieces // 2 + step - 1)
    for k in range(pieces // 2 + count - 1, pieces):
        relay(k)
    for copy in weights + over:
        copy.wait_send()
    for copy in locals_ + streams + passed + [beside] + [copy for _, copy in swaps]:
        copy.wait()

    @pl.when((mine == group - 1) & (block < count - 1))
    def _():
        for there in range(group):
            halo_copy(there).wait_send()

    @pl.when(block > 0)
    def _():
        halo_copy(0).wait_recv()


def tree_sum(parts):
    parts = list(parts)
    while len(parts) > 1:
        parts = [
            parts[k] + parts[k + 1] if k + 1 < len(parts) else parts[k]
            for k in range(0, len(parts), 2)
        ]
    return parts[0]


def scan_kernel(
    group, count, rows_dp, x_ref, up_ref, taps_row, factor_row, coef_row, rate_row, norm_ref,
    go_ref, wg_ref, yo_ref, so_ref, taps_ref, factor_ref, coef_ref,
    shaped, mixed, gradf, gext, starts, bstarts, states, hsend, hrecv,
    gated_ref, gated_t, small_ref, wp_ref, y_ref,
    wbuf, pair, qbuf, qsum, qz, qpair, sbuf,
    ss, sr, hss, hsr, wsend, wrecv, ysend, yrecv, ssend, srecv, tsend, trecv, psend, precv,
    qsend, qrecv, zsend, zrecv, fsend, frecv, own,
):
    me = lax.axis_index("ctx")
    line = lax.axis_index("dp")
    mine, block = lax.rem(me, group), lax.div(me, group)
    steps = up_ref.shape[0]
    width = up_ref.shape[2]
    modes = factor_ref.shape[0]
    greet_all(group * count, rows_dp)
    for m in range(modes):
        factor_ref[m] = jnp.broadcast_to(factor_row[m : m + 1], (CHUNKS, width))
        coef_ref[m] = jnp.broadcast_to(coef_row[m : m + 1], (CHUNKS, width))
    for i in range(3):
        for j in range(7):
            taps_ref[i, j] = jnp.broadcast_to(taps_row[i, j : j + 1], (CHUNKS, width))
    row = lax.broadcasted_iota(jnp.int32, (CHUNKS, LANES), 0)
    spans = [slice(k, k + LANES) for k in range(0, width, LANES)]

    def down(v):
        return jnp.where(row > 0, pltpu.roll(v, 1, 0), 0.0)

    def up(v):
        return jnp.where(row < CHUNKS - 1, pltpu.roll(v, CHUNKS - 1, 0), 0.0)

    zeros = tuple(jnp.zeros((CHUNKS, LANES), jnp.float32) for _ in range(modes))
    for span in spans:

        def first(s, state):
            made = []
            for i in range(3):
                total = tree_sum(
                    [taps_ref[i, j, :, span] * x_ref[i, s + HALO - j, :, span] for j in range(7)]
                )
                shaped[i, s, :, span] = total
                made.append(total)
            value = made[1] * made[2]
            mixed[s, :, span] = value
            gradf[s, :, span] = up_ref[s, :, span] * made[0]
            return tuple(factor_ref[m, :, span] * state[m] + value for m in range(modes))

        ends = lax.fori_loop(0, steps, first, zeros)

        def first_back(k, state):
            value = gradf[steps - 1 - k, :, span]
            return tuple(factor_ref[m, :, span] * state[m] + value for m in range(modes))

        firsts = lax.fori_loop(0, steps, first_back, zeros)
        for m in range(modes):
            fs = jnp.broadcast_to(
                jnp.exp(-rate_row[m : m + 1, span] * float(steps)), (CHUNKS, LANES)
            )
            a = jnp.zeros((CHUNKS, LANES), jnp.float32)
            b = a
            for _ in range(CHUNKS - 1):
                a = down(fs * a + ends[m])
                b = up(fs * b + firsts[m])
            starts[m, :, span] = a
            bstarts[m, :, span] = b
            states[block, 0, m : m + 1, span] = (fs * a + ends[m])[CHUNKS - 1 :]
            states[block, 1, m : m + 1, span] = (fs * b + firsts[m])[:1]

    copies = [
        remote(
            states.at[block],
            states.at[block],
            ss.at[step],
            sr.at[step],
            lax.rem(block + step, count) * group + mine,
        )
        for step in range(1, count)
    ]
    for copy in copies:
        copy.start()
    for copy in copies:
        copy.wait()
    incoming = jnp.zeros((modes, width), jnp.float32)
    outgoing = incoming
    decay = jnp.exp(-rate_row[...] * float(steps * CHUNKS))
    place = row.astype(jnp.float32) * float(steps)
    for k in range(count):
        incoming = jnp.where(k < block, decay * incoming + states[k, 0], incoming)
        r = count - 1 - k
        outgoing = jnp.where(r > block, decay * outgoing + states[r, 1], outgoing)
    for span in spans:
        for m in range(modes):
            rate = rate_row[m : m + 1, span]
            starts[m, :, span] += jnp.exp(-rate * place) * incoming[m : m + 1, span]
            far = float(steps * (CHUNKS - 1)) - place
            bstarts[m, :, span] += jnp.exp(-rate * far) * outgoing[m : m + 1, span]

    for span in spans:

        def second(s, state):
            value = mixed[s, :, span]
            new = tuple(factor_ref[m, :, span] * state[m] + value for m in range(modes))
            filtered = tree_sum([coef_ref[m, :, span] * new[m] for m in range(modes)])
            gated_ref[s, :, span] = shaped[0, s, :, span] * filtered
            gext[0, s, :, span] = up_ref[s, :, span] * filtered
            return new

        lax.fori_loop(0, steps, second, tuple(starts[m, :, span] for m in range(modes)))
        gated_t[span, :] = jnp.swapaxes(
            jnp.swapaxes(gated_ref[:, :, span], 0, 1).reshape(steps * CHUNKS, LANES), 0, 1
        ).astype(gated_t.dtype)

    f32 = jnp.float32
    half = pair.shape[2]
    part = qpair.shape[3]
    tile = math.gcd(part, 512)
    members = count * rows_dp
    slot = block * rows_dp + line
    smalls = []
    for step in range(1, members):
        there = lax.rem(slot + step, members)
        smalls.append(
            remote(
                small_ref,
                sbuf.at[slot],
                ssend.at[step],
                srecv.at[step],
                lax.div(there, rows_dp) * group + mine,
                lax.rem(there, rows_dp),
            )
        )
    weights = []
    for step in range(1, count):
        there = lax.rem(block + step, count)
        to = there * group + mine
        weights.append(
            remote(
                wp_ref.at[there, :, pl.ds(0, half)], wbuf.at[step], wsend.at[step],
                wrecv.at[step], to,
            )
        )
    pairs = []
    quarters, finals = [[] for _ in range(ROUNDS)], [[] for _ in range(ROUNDS)]
    sums = [[] for _ in range(ROUNDS)]
    for step in range(1, rows_dp):
        to = lax.rem(line + step, rows_dp)
        pairs.append(
            remote(pair.at[line], pair.at[line], psend.at[step], precv.at[step], me, to)
        )
        for q in range(ROUNDS):
            begin = half + q * rows_dp * part
            columns = pl.ds(pl.multiple_of(begin + to * part, part), part)
            at = q * rows_dp + step
            quarters[q].append(
                remote(
                    wp_ref.at[:, :, columns], qbuf.at[q, step], qsend.at[at], qrecv.at[at],
                    me, to,
                )
            )
            held = qpair.at[q, line]
            finals[q].append(remote(held, held, fsend.at[at], frecv.at[at], me, to))
    for step in range(1, count):
        there = lax.rem(block + step, count)
        for q in range(ROUNDS):
            at = q * count + step
            sums[q].append(
                remote(
                    qsum.at[q, there], qz.at[q, step], zsend.at[at], zrecv.at[at],
                    there * group + mine,
                )
            )
    outs, totals = [], []
    for step in range(1, group):
        there = lax.rem(mine + step, group)
        to = block * group + there
        outs.append(
            remote(y_ref.at[there], yo_ref.at[mine], ysend.at[step], yrecv.at[step], to)
        )
        totals.append(
            remote(so_ref.at[mine], so_ref.at[mine], tsend.at[step], trecv.at[step], to)
        )
    def each(width, body):
        def run(k, nothing):
            body(pl.multiple_of(k * tile, tile))
            return nothing

        lax.fori_loop(0, width // tile, run, 0)


    own_rows = wp_ref.shape[1]

    def product(at):
        at = pl.ds(at, tile)
        value = jnp.dot(gated_t[...], go_ref[:, at], preferred_element_type=f32)
        value = value.astype(wp_ref.dtype)
        for k in range(count):
            wp_ref[k, :, at] = value[k * own_rows : (k + 1) * own_rows]

    for q in (0, ROUNDS) + tuple(range(1, ROUNDS)):
        begin = half + q * rows_dp * part if q < ROUNDS else 0
        each(half, lambda at: product(pl.multiple_of(begin + at, tile)))
        for copy in quarters[q] if q < ROUNDS else weights:
            copy.start()

    for span in spans:

        def second_back(k, carry):
            state, total = carry
            s = steps - 1 - k
            value = gradf[s, :, span]
            other = mixed[s, :, span]
            new = tuple(factor_ref[m, :, span] * state[m] + value for m in range(modes))
            total = tuple(total[m] + other * new[m] for m in range(modes))
            grad = tree_sum([coef_ref[m, :, span] * new[m] for m in range(modes)])
            gext[1, s, :, span] = grad * shaped[2, s, :, span]
            gext[2, s, :, span] = grad * shaped[1, s, :, span]
            return new, total

        _, total = lax.fori_loop(
            0, steps, second_back, (tuple(bstarts[m, :, span] for m in range(modes)), zeros)
        )
        for m in range(modes):
            small_ref[21 + m : 22 + m, span] = norm_ref[m : m + 1, span] * jnp.sum(
                total[m], axis=0, keepdims=True
            )
    if small_ref.shape[0] > 21 + modes:
        small_ref[21 + modes :, :] = jnp.zeros(
            (small_ref.shape[0] - 21 - modes, width), jnp.float32
        )

    for i in range(3):
        for s in range(HALO):
            hsend[i, s : s + 1, :] = gext[i, s, 0:1, :]
    ahead = remote(
        hsend, hrecv, hss.at[0], hsr.at[0], jnp.maximum(block - 1, 0) * group + mine
    )

    @pl.when(block > 0)
    def _():
        ahead.start()

    for span in spans:
        for i in range(3):

            def tap(s, sums):
                value = gext[i, s, :, span]
                return tuple(
                    sums[j] + value * x_ref[i, s + HALO - j, :, span] for j in range(7)
                )

            tapped = lax.fori_loop(0, steps, tap, zeros[:7], unroll=2)
            for j in range(7):
                at = i * 7 + j
                small_ref[at : at + 1, span] = jnp.sum(tapped[j], axis=0, keepdims=True)

    sbuf[slot] = small_ref[...]
    for copy in smalls:
        copy.start()
    def gather_rows(q):
        for copy in quarters[q]:
            copy.wait()

        def add_rows(at):
            begin = half + q * rows_dp * part
            source = pl.ds(pl.multiple_of(begin + line * part + at, tile), tile)
            at = pl.ds(at, tile)
            for k in range(count):
                value = wp_ref[k, :, source].astype(f32)
                for step in range(1, rows_dp):
                    value = value + qbuf[q, step, k, :, at].astype(f32)
                qsum[q, k, :, at] = value.astype(qsum.dtype)

        each(part, add_rows)
        for copy in sums[q]:
            copy.start()

    for q in range(ROUNDS - 1):
        gather_rows(q)

    @pl.when(block == count - 1)
    def _():
        hrecv[...] = jnp.zeros_like(hrecv)

    @pl.when(block > 0)
    def _():
        ahead.wait_send()

    @pl.when(block < count - 1)
    def _():
        ahead.wait_recv()

    for span in spans:
        for i in range(3):
            for s in range(HALO):
                gext[i, steps + s, :, span] = jnp.where(
                    row < CHUNKS - 1,
                    pltpu.roll(gext[i, s, :, span], CHUNKS - 1, 0),
                    hrecv[i, s : s + 1, span],
                )

            def out(s, nothing):
                shaped[i, s, :, span] = tree_sum(
                    [taps_ref[i, j, :, span] * gext[i, s + j, :, span] for j in range(7)]
                )
                return nothing

            lax.fori_loop(0, steps, out, 0, unroll=2)
            value = jnp.swapaxes(shaped[i, :, :, span], 0, 1).astype(y_ref.dtype)
            y_ref[:, i, :, span] = value.reshape(group, y_ref.shape[2], LANES)

    for q in range(ROUNDS - 1, ROUNDS):
        gather_rows(q)
    for copy in outs:
        copy.start()
    keep = pltpu.make_async_copy(y_ref.at[mine], yo_ref.at[mine], own.at[0])
    keep.start()
    for copy in smalls:
        copy.wait()
    total = sbuf[0]
    for k in range(1, members):
        total = total + sbuf[k]
    so_ref[mine] = total
    for copy in totals:
        copy.start()
    for copy in weights:
        copy.wait()

    def add(at):
        at = pl.ds(at, tile)
        value = wp_ref[block, :, at].astype(f32)
        for step in range(1, count):
            value = value + wbuf[step, :, at].astype(f32)
        pair[line, :, at] = value.astype(pair.dtype)

    each(half, add)
    for copy in pairs:
        copy.start()
    def gather_blocks(q):
        for copy in sums[q]:
            copy.wait()

        def add_blocks(at):
            at = pl.ds(at, tile)
            value = qsum[q, block, :, at].astype(f32)
            for step in range(1, count):
                value = value + qz[q, step, :, at].astype(f32)
            qpair[q, line, :, at] = value.astype(qpair.dtype)

        each(part, add_blocks)
        for copy in finals[q]:
            copy.start()

    for q in range(ROUNDS):
        gather_blocks(q)
    for copy in pairs:
        copy.wait()

    def finish(at):
        at = pl.ds(at, tile)
        value = pair[0, :, at].astype(f32)
        for other in range(1, rows_dp):
            value = value + pair[other, :, at].astype(f32)
        wg_ref[:, at] = value

    each(half, finish)
    for q in range(ROUNDS):
        for copy in finals[q]:
            copy.wait()
        for other in range(rows_dp):

            def finish_part(at):
                begin = half + (q * rows_dp + other) * part
                to = pl.ds(pl.multiple_of(begin + at, tile), tile)
                wg_ref[:, to] = qpair[q, other, :, pl.ds(at, tile)].astype(f32)

            each(part, finish_part)
    keep.wait()
    for copy in outs + totals:
        copy.wait()


VMEM = pl.BlockSpec(memory_space=pltpu.VMEM)
DMA = pltpu.SemaphoreType.DMA


def params(number):
    return pltpu.CompilerParams(
        collective_id=number, has_side_effects=True, vmem_limit_bytes=56 * 1024 * 1024
    )


def shards(
    query_proj, key_proj, value_proj, grad_out, out_weight, short_taps, residues, decay_rate
):
    devices, rows_dp = lax.axis_size("ctx"), lax.axis_size("dp")
    group = math.gcd(devices, 4)
    count = devices // group
    mine = lax.rem(lax.axis_index("ctx"), group)
    tokens, channels = query_proj.shape[1:]
    own_rows, columns = out_weight.shape
    width = count * own_rows
    modes = residues.shape[1]
    span_tokens = group * tokens
    steps = span_tokens // CHUNKS
    f32, bf16 = jnp.float32, jnp.bfloat16
    half = columns // (ROUNDS + 1)
    part = half // rows_dp

    def parted(v):
        v = v.reshape(v.shape[:-1] + (count, group, own_rows))
        return jnp.moveaxis(v, -2, 0).reshape((group,) + v.shape[:-3] + (width,))

    def picked(v):
        return lax.dynamic_index_in_dim(parted(v), mine, 0, keepdims=False)

    streams = parted(jnp.stack([query_proj[0], key_proj[0], value_proj[0]]))
    xg, gog, wg, halo = pl.pallas_call(
        functools.partial(gather_kernel, group, count, rows_dp),
        out_shape=(
            jax.ShapeDtypeStruct((group, 3, tokens, width), bf16),
            jax.ShapeDtypeStruct((group, tokens, columns), bf16),
            jax.ShapeDtypeStruct((count, own_rows, columns), bf16),
            jax.ShapeDtypeStruct((3, 16, width), bf16),
        ),
        in_specs=[VMEM] * 3,
        out_specs=(VMEM,) * 4,
        scratch_shapes=[
            DMA((group,)), DMA((group,)), DMA((PIECES,)), DMA((PIECES,)),
            DMA((PIECES,)), DMA((PIECES,)), DMA((1,)), DMA((1,)),
            DMA((count,)), DMA((count,)), DMA((count * rows_dp,)), DMA((count * rows_dp,)),
            DMA((group,)), DMA((1,)), DMA((3,)),
        ],
        compiler_params=params(0),
        name="gather",
    )(streams, grad_out[0], out_weight)

    out_rows = gog.reshape(span_tokens, columns)
    upstream = lax.dot_general(
        out_rows,
        wg.reshape(width, columns),
        (((1,), (1,)), ((), ())),
        preferred_element_type=f32,
    )
    upstream = jnp.swapaxes(upstream.reshape(CHUNKS, steps, width), 0, 1)
    whole = jnp.swapaxes(xg, 0, 1).reshape(3, CHUNKS, steps, width)
    before = jnp.concatenate(
        [halo[:, None, 16 - HALO :], whole[:, :-1, steps - HALO :]], axis=1
    )
    extended = jnp.swapaxes(jnp.concatenate([before, whole], axis=2), 1, 2).astype(f32)

    tables = picked(
        jnp.concatenate(
            [
                jnp.swapaxes(short_taps, 1, 2).reshape(21, channels),
                residues.T,
                decay_rate.T,
            ]
        )
    )
    taps = tables[:21].reshape(3, 7, width)
    rate = tables[21 + modes :]
    norm = jnp.sqrt(-jnp.expm1(-2.0 * rate))
    coef = tables[21 : 21 + modes] * norm
    tall = (21 + modes + 7) // 8 * 8
    small = (tall, width)
    weight_grad, yo, so = pl.pallas_call(
        functools.partial(scan_kernel, group, count, rows_dp),
        out_shape=(
            jax.ShapeDtypeStruct((own_rows, columns), f32),
            jax.ShapeDtypeStruct((group, 3, tokens, width), bf16),
            jax.ShapeDtypeStruct((group,) + small, f32),
        ),
        in_specs=[VMEM] * 8,
        out_specs=(VMEM,) * 3,
        scratch_shapes=[
            pltpu.VMEM((3, 7, CHUNKS, width), f32),
            pltpu.VMEM((modes, CHUNKS, width), f32),
            pltpu.VMEM((modes, CHUNKS, width), f32),
            pltpu.VMEM((3, steps, CHUNKS, width), f32),
            pltpu.VMEM((steps, CHUNKS, width), f32),
            pltpu.VMEM((steps, CHUNKS, width), f32),
            pltpu.VMEM((3, steps + HALO, CHUNKS, width), f32),
            pltpu.VMEM((modes, CHUNKS, width), f32),
            pltpu.VMEM((modes, CHUNKS, width), f32),
            pltpu.VMEM((count, 2, modes, width), f32),
            pltpu.VMEM((3, HALO, width), f32),
            pltpu.VMEM((3, HALO, width), f32),
            pltpu.VMEM((steps, CHUNKS, width), f32),
            pltpu.VMEM((width, span_tokens), bf16),
            pltpu.VMEM(small, f32),
            pltpu.VMEM((count, own_rows, columns), bf16),
            pltpu.VMEM((group, 3, tokens, width), bf16),
            pltpu.VMEM((count, own_rows, half), bf16),
            pltpu.VMEM((rows_dp, own_rows, half), bf16),
            pltpu.VMEM((ROUNDS, rows_dp, count, own_rows, part), bf16),
            pltpu.VMEM((ROUNDS, count, own_rows, part), bf16),
            pltpu.VMEM((ROUNDS, count, own_rows, part), bf16),
            pltpu.VMEM((ROUNDS, rows_dp, own_rows, part), bf16),
            pltpu.VMEM((count * rows_dp,) + small, f32),
            DMA((count,)), DMA((count,)), DMA((1,)), DMA((1,)),
            DMA((count,)), DMA((count,)), DMA((group,)), DMA((group,)),
            DMA((count * rows_dp,)), DMA((count * rows_dp,)),
            DMA((group,)), DMA((group,)), DMA((rows_dp,)), DMA((rows_dp,)),
            DMA((ROUNDS * rows_dp,)), DMA((ROUNDS * rows_dp,)),
            DMA((ROUNDS * count,)), DMA((ROUNDS * count,)),
            DMA((ROUNDS * rows_dp,)), DMA((ROUNDS * rows_dp,)), DMA((1,)),
        ],
        compiler_params=params(1),
        name="scan",
    )(extended, upstream, taps, jnp.exp(-rate), coef, rate, norm, out_rows)

    def joined(v):
        v = v.reshape(v.shape[:-1] + (count, own_rows))
        v = jnp.moveaxis(v, 0, -2)
        return v.reshape(v.shape[:-3] + (channels,))

    grads = joined(yo)
    sums = joined(so)
    taps_grad = jnp.swapaxes(sums[:21].reshape(3, 7, channels), 1, 2)
    residue_grad = sums[21 : 21 + modes].T
    return (grads[0][None], grads[1][None], grads[2][None], weight_grad, taps_grad, residue_grad)


def solution(mesh):
    placed = (
        P("dp", "ctx", None),
        P("dp", "ctx", None),
        P("dp", "ctx", None),
        P("dp", "ctx", None),
        P("ctx", None),
        P(),
        P(),
        P(),
    )
    return jax.shard_map(
        shards,
        mesh=mesh,
        in_specs=placed,
        out_specs=(
            P("dp", "ctx", None),
            P("dp", "ctx", None),
            P("dp", "ctx", None),
            P("ctx", None),
            P(),
            P(),
        ),
        check_vma=False,
    )
```
